256 devices in a mesh: group: 4 (over x), sub: 64 (over z, y, core).
Axes of the slice: x: 4, y: 4, z: 8, core: 2. Of those that a mesh axis runs over, the one named last changes fastest.
Arguments:
- load_cases: bfloat16 [4, 64, 1536, 256], P('group', 'sub'), may hold values from -6 to 6
- inv_schur: bfloat16 [4, 64, 1536, 1536], P('group', 'sub'), may hold values from -0.15625 to 0.15625
- schur_blocks: bfloat16 [4, 64, 1536, 1536], P('group', 'sub'), may hold values from -0.15625 to 0.15625
- coarse_basis: float32 [4, 64, 1536], P('group', 'sub'), may hold values from -0.53033006 to 0.53033006
- coarse_map: int32 [4, 64, 12], P('group', 'sub'), may hold values from 0 to 1023
- multiplicity: int32 [4, 64, 12], P('group', 'sub'), may hold values from 2 to 4
- recv_code: int32 [4, 64, 12], P('group', 'sub'), may hold values from 0 to 23, as said below
- send_blocks: int32 [4, 64, 24], P('group', 'sub'), may hold values from -1 to 11, as said below
- coarse_inv: float32 [4, 1024, 1024], P('group', 'sub'), may hold values from -0.1875 to 0.1875
Outputs:
- multipliers: float32 [4, 64, 1536, 256], P('group', 'sub')
The draws below stay inside these ranges and needn't reach their ends.
Inputs may be any that keep to these rules, and one draw needn't show every extreme that they name: `recv_code`: within one subdomain the blocks read distinct codes; in every subdomain all 4 slots of one direction are read. `send_blocks`: entry d * 4 + j is the block a subdomain sends as slot j of direction d, to the subdomain that reads direction d from it; it is -1 exactly where that subdomain reads nothing from the slot.
All inputs are finite; a program needn't handle non-finite values.
Results may differ from the reference program's by a relative error of at most 0.0085.
Values may be sent and summed in bfloat16 or wider, within the bound.
A program may use at most 64 MiB of HBM per device.

```python
import jax
import jax.numpy as jnp
from jax import lax

NB = 1536
BLK = 128
NBLK = 12
DIRS = 6
CAP = 4
NC = 1024
CASES = 256
ITERS = 2
NGROUP = 4
NSUBD = 64


SHIFTS = ((1, 1), (1, -1), (1, 2), (1, -2), (0, 1), (0, -1))


def neighbour_tables(key):
    seed_key = jax.random.fold_in(key, 4242)
    full_key, order_key, block_key, remote_key = jax.random.split(seed_key, 4)
    devices_all = NGROUP * NSUBD
    slot_total = DIRS * CAP
    code_ids = jnp.arange(slot_total, dtype=jnp.int32)
    full_dir = jax.random.randint(full_key, (devices_all, 1), 0, DIRS, dtype=jnp.int32)
    priority = jax.random.randint(order_key, (devices_all, slot_total), 0, 1 << 20, dtype=jnp.int32) * slot_total + code_ids[None, :]
    priority = jnp.where(code_ids[None, :] // CAP == full_dir, code_ids[None, :] - slot_total, priority)
    ranking = jnp.argsort(priority, axis=1, stable=True).astype(jnp.int32)
    chosen = ranking[:, :NBLK]
    block_ids = jnp.arange(NBLK, dtype=jnp.int32)
    shuffle_scores = jax.random.randint(block_key, (devices_all, NBLK), 0, 1 << 20, dtype=jnp.int32) * NBLK + block_ids[None, :]
    shuffle = jnp.argsort(shuffle_scores, axis=1, stable=True).astype(jnp.int32)
    recv_flat = jnp.take_along_axis(chosen, shuffle, axis=1)
    used = jnp.sum((chosen[:, :, None] == code_ids[None, None, :]).astype(jnp.int32), axis=1) > 0
    remote = jax.random.randint(remote_key, (devices_all, slot_total), 0, NBLK, dtype=jnp.int32)
    wanted = jnp.where(used, remote, -1).reshape(NGROUP, NSUBD, DIRS, CAP)
    parts = []
    for direction in range(DIRS):
        axis_pos, offset = SHIFTS[direction]
        parts.append(jnp.roll(wanted[:, :, direction], -offset, axis=axis_pos))
    sending = jnp.stack(parts, axis=2).reshape(NGROUP, NSUBD, slot_total)
    return (recv_flat.reshape(NGROUP, NSUBD, NBLK), sending)


def draw_recv_code(key, part):
    return neighbour_tables(key)[0]


def draw_send_blocks(key, part):
    return neighbour_tables(key)[1]


def with_ends(drawn, key, low, largest):
    place = [jax.random.randint(jax.random.fold_in(key, axis), (), 0, length) for axis, length in enumerate(drawn.shape)]
    widest = drawn.shape.index(max(drawn.shape))
    beside = place[:widest] + [(place[widest] + 1) % drawn.shape[widest]] + place[widest + 1:]
    return drawn.at[tuple(place)].set(low).at[tuple(beside)].set(largest)


def steps_of(rng, shape, cuts, low, largest):
    factor_of, own = 1.0, jax.random.fold_in(rng, 6)
    for dim, blocks in cuts:
        draws = jnp.exp(jax.random.uniform(jax.random.fold_in(own, dim), (blocks,), jnp.float32, low / len(cuts), largest / len(cuts)))
        factor_of = factor_of * jnp.repeat(draws, shape[dim] // blocks).reshape([-1 if axis == dim else 1 for axis in range(len(shape))])
    return factor_of


def gaussian(stream_key, extent, deviation, bound, cuts=(), held_as=jnp.bfloat16):
    entries = jax.random.normal(stream_key, extent, jnp.float32) * deviation
    if len(cuts) > 0:
        entries = steps_of(stream_key, extent, cuts, -0.22, 0.18) * entries
    return jnp.clip(entries, min=-bound, max=bound).astype(held_as)


def setup_inputs(seed: int = 0) -> dict:
    splits = jax.random.split(jax.random.key(seed), 10)
    return {
        "load_cases": gaussian(splits[0], (NGROUP, NSUBD, NB, CASES), 1.0, 6.0, ((0, 4), (1, 64))),
        "inv_schur": gaussian(splits[1], (NGROUP, NSUBD, NB, NB), NB ** -0.5, 0.15625, ((0, 4), (1, 64))),
        "schur_blocks": gaussian(splits[2], (NGROUP, NSUBD, NB, NB), NB ** -0.5, 0.15625, ((0, 4), (1, 64))),
        "coarse_basis": gaussian(splits[3], (NGROUP, NSUBD, NB), (2.0 / BLK ** 0.5), 0.53033006, ((0, 4), (1, 64)), jnp.float32),
        "coarse_map": with_ends(jax.random.randint(splits[4], (NGROUP, NSUBD, NBLK), 0, NC), jax.random.fold_in(splits[4], 1), 0, NC - 1).astype(jnp.int32),
        "multiplicity": with_ends(jax.random.randint(splits[5], (NGROUP, NSUBD, NBLK), 2, 5), jax.random.fold_in(splits[5], 1), 2, 4).astype(jnp.int32),
        "recv_code": draw_recv_code(jax.random.fold_in(splits[9], 71), 0),
        "send_blocks": draw_send_blocks(jax.random.fold_in(splits[9], 71), 0),
        "coarse_inv": gaussian(splits[8], (NGROUP, NC, NC), NC ** -0.5, 0.1875, ((0, 4), (1, 64)), jnp.float32),
    }


SHIFTS = ((1, 1), (1, -1), (1, 2), (1, -2), (0, 1), (0, -1))
HIGHEST = lax.Precision.HIGHEST


def jump(values, recv_code, send_blocks):
    pieces = []
    for direction in range(DIRS):
        axis_pos, offset = SHIFTS[direction]
        wanted = send_blocks[:, :, direction * CAP:(direction + 1) * CAP]
        picked = jnp.take_along_axis(values, jnp.maximum(wanted, 0)[:, :, :, None, None], axis=2)
        picked = jnp.where((wanted >= 0)[:, :, :, None, None], picked, jnp.zeros((), jnp.bfloat16))
        pieces.append(jnp.roll(picked, offset, axis=axis_pos))
    received = jnp.concatenate(pieces, axis=2)
    remote = jnp.take_along_axis(received, recv_code[:, :, :, None, None], axis=2)
    return values.astype(jnp.float32) - remote.astype(jnp.float32)


def local_products(matrices, vectors):
    flat_mats = matrices.reshape(NGROUP * NSUBD, NB, NB)
    flat_vecs = vectors.reshape(NGROUP * NSUBD, NB, CASES)
    result = lax.map(lambda pair: jnp.dot(pair[0], pair[1], preferred_element_type=jnp.float32), (flat_mats, flat_vecs))
    return result.reshape(NGROUP, NSUBD, NBLK, BLK, CASES)


def reference(load_cases, inv_schur, schur_blocks, coarse_basis, coarse_map, multiplicity, recv_code, send_blocks, coarse_inv):
    weights = (1.0 / multiplicity.astype(jnp.float32))[:, :, :, None, None]
    basis_rows = coarse_basis.reshape(NGROUP, NSUBD, NBLK, BLK)
    selector = (coarse_map[:, :, :, None] == jnp.arange(NC, dtype=jnp.int32)[None, None, None, :]).astype(jnp.float32)
    multipliers = jnp.zeros((NGROUP, NSUBD, NB, CASES), jnp.float32)
    for iteration in range(ITERS):
        residual_load = (load_cases.astype(jnp.float32) - multipliers).astype(jnp.bfloat16)
        displacement = local_products(inv_schur, residual_load)
        projected = jnp.sum(basis_rows[:, :, :, :, None] * displacement, axis=3)
        coarse_resid = jnp.einsum("gsbk,gsbc->gkc", selector, projected, precision=HIGHEST)
        coarse = jnp.einsum("gjk,gjc->gkc", coarse_inv, coarse_resid, precision=HIGHEST)
        coarse_here = jnp.einsum("gsbk,gkc->gsbc", selector, coarse, precision=HIGHEST)
        corrected = (displacement + basis_rows[:, :, :, :, None] * coarse_here[:, :, :, None, :]).astype(jnp.bfloat16)
        scaled = (jump(corrected, recv_code, send_blocks) * weights).astype(jnp.bfloat16)
        dirichlet = local_products(schur_blocks, scaled)
        dual_step = (dirichlet * weights).astype(jnp.bfloat16)
        multipliers = multipliers + jump(dual_step, recv_code, send_blocks).reshape(NGROUP, NSUBD, NB, CASES)
    return multipliers
```

```python
import functools

import jax
import jax.numpy as jnp
from jax import lax
from jax.experimental import pallas as pl
from jax.experimental.pallas import tpu as pltpu
from jax.sharding import PartitionSpec as P

BLK = 128
DIRS = 6
CAP = 4
ITERS = 2
SLOTS = DIRS * CAP
PAD = 16
CH = 2
CORES = 2
TILE = 256
OFFSETS = (1, -1, 2, -2)
ORDER = (2, 3, 0, 1, 4, 5)
MESH = pl.DeviceIdType.MESH
BF = jnp.bfloat16
F32 = jnp.float32


def kernel(
    zs, ys, gs,
    load_hbm, a_hbm, s_hbm, basis_ref, cinv_ref, map_ref, mult_ref, code_ref, send_ref,
    out_hbm,
    load_v, a_v, s_v, load_sem, a_sem, s_sem, out_sem,
    bcol, brcol, brow, bslab, brecv, bs_sem, br_sem,
    mown, mrow, mtile, mall, ms_sem, mr_sem, zs_sem, zr_sem,
    onehot, selbuf, colz, colall, cs_sem, cr_sem, ys_sem, yr_sem, wbuf,
    x, slab, rv0, rv1, rv2, rv3, rv4, rv5, rv6, rv7, es_sem, er_sem,
    sc, mul, res,
    pf, psend, prow, pall, ps_sem, pr_sem, qs_sem, qr_sem,
    crow, cout, cin, cloc, ks_sem, kr_sem, cslab, cv0, cv1, cv2, cv3, ts_sem, tr_sem,
):
    nb, cases = load_v.shape
    nblk = nb // BLK
    cw = cases // CH
    rows = zs * ys * CORES
    rowdev = ys * CORES
    recv = (rv0, rv1, rv2, rv3, rv4, rv5, rv6, rv7)
    crecv = (cv0, cv1, cv2, cv3)
    g = lax.axis_index("group")
    s = lax.axis_index("sub")
    c = lax.rem(s, CORES)
    zy = lax.div(s, CORES)
    y = lax.rem(zy, ys)
    z = lax.div(zy, ys)
    yc = y * CORES + c

    def sub_at(zz, yy, cc):
        return (zz * ys + yy) * CORES + cc

    def row_peer(dy, dc):
        yy = lax.rem(y + dy, ys)
        cc = lax.rem(c + dc, CORES)
        return (g, sub_at(z, yy, cc))

    def col_peer(dz):
        return (g, sub_at(lax.rem(z + dz, zs), y, c))

    def reader(d):
        if d < 4:
            return (g, lax.rem(s + OFFSETS[d] + rows, rows))
        return (lax.rem(g + (1 if d == 4 else gs - 1), gs), s)

    row_steps = [(dy, dc) for dy in range(ys) for dc in range(CORES) if (dy, dc) != (0, 0)]
    col_steps = list(range(1, zs))
    started = []

    def remote(src, dst, ssem, rsem, dev):
        return pltpu.make_async_remote_copy(
            src_ref=src, dst_ref=dst, send_sem=ssem, recv_sem=rsem,
            device_id=dev, device_id_type=MESH,
        )

    barrier = pltpu.get_barrier_semaphore()
    peers = [row_peer(dy, dc) for dy, dc in row_steps]
    peers += [col_peer(dz) for dz in col_steps]
    peers += [reader(d) for d in range(DIRS)]
    for peer in peers:
        pl.semaphore_signal(barrier, inc=1, device_id=peer, device_id_type=MESH)
    load_copy = pltpu.make_async_copy(load_hbm.at[0, 0], load_v, load_sem)
    load_copy.start()
    tiles = nb // TILE

    def a_copy(t):
        part = pl.ds(t * TILE, TILE)
        return pltpu.make_async_copy(a_hbm.at[0, 0, part], a_v.at[part], a_sem.at[t])

    for t in range(tiles):
        a_copy(t).start()
    s_copy = pltpu.make_async_copy(s_hbm.at[0, 0], s_v, s_sem)
    s_copy.start()

    lane = lax.broadcasted_iota(jnp.int32, (8, 128), 1)
    mine = jnp.full((8, 128), -1, jnp.int32)
    for b in range(nblk):
        line = basis_ref[:, b * BLK:(b + 1) * BLK]
        brow[b:b + 1, :] = line
        bcol[b] = jnp.transpose(jnp.broadcast_to(line, (BLK, BLK)))
        mine = jnp.where(lane == b, map_ref[0, b], mine)
    mown[...] = mine
    bslab[...] = jnp.zeros_like(bslab)
    for k in range(SLOTS):
        at = (k // CAP) * 8 + k % CAP
        bslab[at:at + 1, :] = brow[pl.ds(jnp.maximum(send_ref[0, k], 0), 1), :]
    pl.semaphore_wait(barrier, len(peers))

    map_row = []
    for n, (dy, dc) in enumerate(row_steps):
        map_row.append(remote(mown, mrow.at[yc], ms_sem.at[n], mr_sem.at[n], row_peer(dy, dc)))
        map_row[-1].start()
    basis_out = []
    for d in range(DIRS):
        part = pl.ds(d * 8, 8)
        basis_out.append(remote(bslab.at[part], brecv.at[part], bs_sem.at[d], br_sem.at[d], reader(d)))
        basis_out[-1].start()
    started += map_row + basis_out
    mrow[yc] = mine

    def slab_copy(e, h, d):
        part = pl.ds(d * CAP, CAP)
        n = (e * CH + h) * DIRS + d
        return remote(
            slab.at[e * CH + h, part], recv[e * CH + h].at[part],
            es_sem.at[n], er_sem.at[n], reader(d),
        )

    def pack(e, h):
        for d in ORDER:
            for j in range(CAP):
                k = d * CAP + j
                slab[e * CH + h, k] = x[h, jnp.maximum(send_ref[0, k], 0)]
            copy = slab_copy(e, h, d)
            copy.start()
            started.append(copy)

    def wait_slabs(e, h):
        for d in ORDER:
            slab_copy(e, h, d).wait_recv()

    def p_send(i, h):
        psend[i, h] = pf[h].astype(BF)
        dc = lax.rem(c + h, CORES)
        for dy in range(ys):
            n = (i * CH + h) * ys + dy
            copy = remote(
                psend.at[i, h], prow.at[i, yc], ps_sem.at[n],
                pr_sem.at[i * rowdev + dy * CORES + dc], row_peer(dy, dc),
            )
            if dy == 0:
                @pl.when(dc != 0)
                def _():
                    copy.start()

                @pl.when(dc == 0)
                def _():
                    prow[i, yc] = pf[h].astype(BF)
            else:
                copy.start()

    def p_wait_sends():
        for i in range(ITERS):
            for h in range(CH):
                dc = lax.rem(c + h, CORES)
                for dy in range(ys):
                    n = (i * CH + h) * ys + dy
                    copy = remote(
                        psend.at[i, h], prow.at[i, yc], ps_sem.at[n],
                        pr_sem.at[i * rowdev + dy * CORES + dc], row_peer(dy, dc),
                    )
                    if dy == 0:
                        @pl.when(dc != 0)
                        def _():
                            copy.wait_send()
                    else:
                        copy.wait_send()

    def q_copy(i, n, dz):
        return remote(
            prow.at[i], pall.at[i, z], qs_sem.at[i * zs + n], qr_sem.at[i * zs + n], col_peer(dz)
        )

    def relay(i):
        for dy, dc in row_steps:
            remote(
                psend.at[i, 0], prow.at[i, 0], ps_sem.at[0],
                pr_sem.at[i * rowdev + dy * CORES + dc], row_peer(dy, dc),
            ).wait_recv()
        for n, dz in enumerate(col_steps):
            q_copy(i, n, dz).start()
        pall[i, z] = prow[i]

    def partner_copy(i):
        return remote(cout.at[i], cin.at[i], ks_sem.at[i], kr_sem.at[i], row_peer(0, 1))

    def coarse(i):
        for n, dz in enumerate(col_steps):
            q_copy(i, n, dz).wait_recv()
        every = pall[i].reshape(rows * PAD, cw)
        crow[...] = jnp.dot(wbuf[...], every, preferred_element_type=F32).reshape(rowdev, PAD, cw)
        cout[i] = crow[y * CORES + (1 - c)]
        partner_copy(i).start()

    def t_copy(i, h, d):
        part = pl.ds(d * 8, 8)
        n = (i * CH + h) * DIRS + d
        return remote(
            cslab.at[i * CH + h, part], crecv[i * CH + h].at[part],
            ts_sem.at[n], tr_sem.at[n], reader(d),
        )

    def spread(i, h):
        @pl.when(c == h)
        def _():
            cloc[h] = crow[yc]

        @pl.when(c != h)
        def _():
            partner_copy(i).wait_recv()
            cloc[h] = cin[i]

        cslab[i * CH + h] = jnp.zeros(cslab.shape[1:], F32)
        for d in range(DIRS):
            for j in range(CAP):
                k = d * CAP + j
                at = d * 8 + j
                cslab[i * CH + h, at:at + 1, :] = cloc[h, pl.ds(jnp.maximum(send_ref[0, k], 0), 1), :]
            copy = t_copy(i, h, d)
            copy.start()
            started.append(copy)

    def code_row(b):
        code = code_ref[0, b]
        return code, (code // CAP) * 8 + code % CAP

    def weight(b):
        return 1.0 / jnp.full((1, 128), mult_ref[0, b].astype(F32))

    def keep(b, h, disp):
        pf[h, pl.ds(b, 1), :] = jnp.sum(bcol[b] * disp, axis=0, keepdims=True)
        x[h, b] = disp.astype(BF)

    per = TILE // BLK

    def first_solve():
        load_copy.wait()

        def step(t, carry):
            a_copy(t).wait()
            acc = jnp.dot(a_v[pl.ds(t * TILE, TILE), :], load_v[...], preferred_element_type=F32)
            for i in range(per):
                for h in range(CH):
                    keep(t * per + i, h, acc[i * BLK:(i + 1) * BLK, h * cw:(h + 1) * cw])
            return carry

        lax.fori_loop(0, tiles, step, 0)

    def solve(h):
        def step(t, carry):
            acc = jnp.dot(a_v[pl.ds(t * TILE, TILE), :], res[h], preferred_element_type=F32)
            for i in range(per):
                keep(t * per + i, h, acc[i * BLK:(i + 1) * BLK])
            return carry

        lax.fori_loop(0, tiles, step, 0)

    def scale(i, h):
        e = 2 * i
        wait_slabs(e, h)
        for d in range(DIRS):
            t_copy(i, h, d).wait_recv()

        def step(b, carry):
            code, at = code_row(b)
            own = x[h, b].astype(F32) + bcol[b] * cloc[h, pl.ds(b, 1), :]
            far = recv[e * CH + h][code].astype(F32) + brcol[b] * crecv[i * CH + h][pl.ds(at, 1), :]
            sc[h, pl.ds(b * BLK, BLK), :] = ((own - far) * weight(b)).astype(BF)
            return carry

        lax.fori_loop(0, nblk, step, 0)

    def dirichlet(h):
        def step(t, carry):
            acc = jnp.dot(s_v[pl.ds(t * TILE, TILE), :], sc[h], preferred_element_type=F32)
            for i in range(per):
                b = t * per + i
                x[h, b] = (acc[i * BLK:(i + 1) * BLK] * weight(b)).astype(BF)
            return carry

        lax.fori_loop(0, tiles, step, 0)

    def update(i, h):
        e = 2 * i + 1
        wait_slabs(e, h)
        cols = slice(h * cw, (h + 1) * cw)

        def step(b, carry):
            part = pl.ds(b * BLK, BLK)
            new = x[h, b].astype(F32) - recv[e * CH + h][code_ref[0, b]].astype(F32)
            if i == 0:
                res[h, part, :] = (load_v[part, cols].astype(F32) - new).astype(BF)
            else:
                new = mul[part, cols] + new
            mul[part, cols] = new
            return carry

        lax.fori_loop(0, nblk, step, 0)

    def column_maps():
        for n in range(len(row_steps)):
            map_row[n].wait_recv()
        line = lax.broadcasted_iota(jnp.int32, (8, 128), 0)
        tile = jnp.full((8, 128), -1, jnp.int32)
        for n in range(rowdev):
            tile = jnp.where(line == n, mrow[n], tile)
        mtile[...] = tile
        copies = []
        for n, dz in enumerate(col_steps):
            copies.append(remote(mtile, mall.at[z], zs_sem.at[n], zr_sem.at[n], col_peer(dz)))
            copies[-1].start()
        mall[z] = tile
        started.extend(copies)
        return copies

    def columns(copies):
        for copy in copies:
            copy.wait_recv()
        grid = jnp.transpose(mall[...].reshape(zs * 8, 128).astype(F32))
        order = rows * PAD
        width = onehot.shape[1]
        ids = lax.broadcasted_iota(jnp.int32, (PAD, width), 1).astype(F32)
        for zz in range(zs):
            for r in range(rowdev):
                at = (zz * rowdev + r) * PAD
                n = zz * 8 + r
                hit = jnp.broadcast_to(grid[:PAD, n:n + 1], (PAD, width)) == ids
                onehot[at:at + PAD, :] = jnp.where(hit, 1.0, 0.0).astype(BF)
        picked = lax.dot_general(
            cinv_ref[0].astype(BF), onehot[...], (((1,), (1,)), ((), ())), preferred_element_type=F32
        ).astype(BF)
        lanes = rowdev * PAD
        copies = []
        for zz in range(zs):
            selbuf[zz] = picked[:, zz * lanes:(zz + 1) * lanes]
        for n, dz in enumerate(col_steps):
            zz = lax.rem(z + dz, zs)
            copies.append(remote(selbuf.at[zz], colz.at[z], cs_sem.at[n], cr_sem.at[n], col_peer(dz)))
            copies[-1].start()
        colz[z] = selbuf[z]
        started.extend(copies)
        return copies

    def share_columns(copies):
        for copy in copies:
            copy.wait_recv()
        out = []
        for n, (dy, dc) in enumerate(row_steps):
            out.append(remote(colz, colall.at[:, yc], ys_sem.at[n], yr_sem.at[n], row_peer(dy, dc)))
            out[-1].start()
        colall[:, yc] = colz[...]
        started.extend(out)
        return out

    def coarse_rows(copies):
        for copy in copies:
            copy.wait_recv()
        mat = colall[...].reshape(onehot.shape[1], rowdev * PAD)
        wide = jnp.dot(onehot[...], mat, preferred_element_type=F32)
        wbuf[...] = jnp.transpose(wide).astype(BF)

    pf[...] = jnp.zeros_like(pf)
    first_solve()
    for h in range(CH):
        p_send(0, h)
    for h in range(CH):
        pack(0, h)
    map_col = column_maps()
    relay(0)
    for copy in basis_out:
        copy.wait_recv()
    for b in range(nblk):
        _, at = code_row(b)
        brcol[b] = jnp.transpose(jnp.broadcast_to(brecv[pl.ds(at, 1), :], (BLK, BLK)))
    col_out = columns(map_col)
    row_out = share_columns(col_out)
    coarse_rows(row_out)
    coarse(0)
    for h in range(CH):
        spread(0, h)
    s_copy.wait()
    for h in range(CH):
        scale(0, h)
        dirichlet(h)
        pack(1, h)
    for h in range(CH):
        update(0, h)
        solve(h)
        p_send(1, h)
        pack(2, h)

        @pl.when(c == h)
        def _():
            relay(1)

    for h in range(CH):
        @pl.when(c == h)
        def _():
            coarse(1)

        spread(1, h)
        scale(1, h)
        dirichlet(h)
        pack(3, h)
    outs = []
    for h in range(CH):
        update(1, h)
        cols = pl.ds(h * cw, cw)
        outs.append(pltpu.make_async_copy(mul.at[:, cols], out_hbm.at[0, 0, :, cols], out_sem.at[h]))
        outs[-1].start()

    for copy in started:
        copy.wait_send()
    p_wait_sends()
    for i in range(ITERS):
        for n, dz in enumerate(col_steps):
            q_copy(i, n, dz).wait_send()
        partner_copy(i).wait_send()
    for copy in outs:
        copy.wait()


def on_device(zs, ys, gs, *args):
    (load_cases, inv_schur, schur_blocks, coarse_basis, coarse_map,
     multiplicity, recv_code, send_blocks, coarse_inv) = args
    _, _, nb, cases = load_cases.shape
    nblk = nb // BLK
    cw = cases // CH
    own, nc = coarse_inv.shape[1:]
    rowdev = ys * CORES
    rows = zs * rowdev
    tiles = nb // TILE
    dma = pltpu.SemaphoreType.DMA
    vm = pltpu.VMEM
    exchanges = 2 * ITERS * CH
    scratch = [
        vm((nb, cases), BF), vm((nb, nb), BF), vm((nb, nb), BF),
        dma, dma((tiles,)), dma, dma((CH,)),
        vm((nblk, BLK, BLK), F32), vm((nblk, BLK, BLK), F32), vm((PAD, BLK), F32),
        vm((DIRS * 8, BLK), F32), vm((DIRS * 8, BLK), F32), dma((DIRS,)), dma((DIRS,)),
        vm((8, 128), jnp.int32), vm((rowdev, 8, 128), jnp.int32), vm((8, 128), jnp.int32),
        vm((zs, 8, 128), jnp.int32), dma((rowdev,)), dma((rowdev,)), dma((zs,)), dma((zs,)),
        vm((rows * PAD, nc), BF), vm((zs, own, rowdev * PAD), BF), vm((zs, own, rowdev * PAD), BF),
        vm((zs, rowdev, own, rowdev * PAD), BF),
        dma((zs,)), dma((zs,)), dma((rowdev,)), dma((rowdev,)), vm((rowdev * PAD, rows * PAD), BF),
        vm((CH, nblk, BLK, cw), BF), vm((exchanges, SLOTS, BLK, cw), BF),
        *[vm((SLOTS, BLK, cw), BF) for _ in range(exchanges)],
        dma((exchanges * DIRS,)), dma((exchanges * DIRS,)),
        vm((CH, nb, cw), BF), vm((nb, cases), F32), vm((CH, nb, cw), BF),
        vm((CH, PAD, cw), F32), vm((ITERS, CH, PAD, cw), BF), vm((ITERS, rowdev, PAD, cw), BF),
        vm((ITERS, zs, rowdev, PAD, cw), BF),
        dma((ITERS * CH * ys,)), dma((ITERS * rowdev,)), dma((ITERS * zs,)), dma((ITERS * zs,)),
        vm((rowdev, PAD, cw), F32), vm((ITERS, PAD, cw), F32), vm((ITERS, PAD, cw), F32),
        vm((CH, PAD, cw), F32), dma((ITERS,)), dma((ITERS,)),
        vm((ITERS * CH, DIRS * 8, cw), F32),
        *[vm((DIRS * 8, cw), F32) for _ in range(ITERS * CH)],
        dma((ITERS * CH * DIRS,)), dma((ITERS * CH * DIRS,)),
    ]
    hbm = pl.BlockSpec(memory_space=pl.ANY)
    inside = pl.BlockSpec(memory_space=pltpu.VMEM)
    scalars = pl.BlockSpec(memory_space=pltpu.SMEM)
    return pl.pallas_call(
        functools.partial(kernel, zs, ys, gs),
        out_shape=jax.ShapeDtypeStruct(load_cases.shape, F32),
        in_specs=[hbm, hbm, hbm, inside, inside, scalars, scalars, scalars, scalars],
        out_specs=hbm,
        scratch_shapes=scratch,
        compiler_params=pltpu.CompilerParams(
            collective_id=0, has_side_effects=True, vmem_limit_bytes=60 * 1024 * 1024
        ),
        name="feti",
    )(
        load_cases, inv_schur, schur_blocks, coarse_basis[0], coarse_inv,
        coarse_map[0], multiplicity[0], recv_code[0], send_blocks[0],
    )


def build(mesh, zs, ys):
    wide = P("group", "sub", None, None)
    thin = P("group", "sub", None)
    return jax.shard_map(
        functools.partial(on_device, zs, ys, mesh.shape["group"]),
        mesh=mesh,
        in_specs=(wide, wide, wide, thin, thin, thin, thin, thin, thin),
        out_specs=wide,
        check_vma=False,
    )


def solution(mesh):
    ys = 4
    return build(mesh, mesh.shape["sub"] // (ys * CORES), ys)
```

```python
import functools

import jax
import jax.numpy as jnp
from jax import lax
from jax.experimental import pallas as pl
from jax.experimental.pallas import tpu as pltpu
from jax.sharding import PartitionSpec as P

BLK = 128
DIRS = 6
CAP = 4
ITERS = 2
SLOTS = DIRS * CAP
PAD = 16
CH = 2
CORES = 2
TILE = 256
OFFSETS = (1, -1, 2, -2)
ALONG = (2, 3, 0, 1)
ACROSS = (4, 5)
ORDER = ALONG + ACROSS
MESH = pl.DeviceIdType.MESH
BF = jnp.bfloat16
F32 = jnp.float32


def kernel(
    zs, ys, gs,
    load_hbm, a_hbm, s_hbm, basis_hbm, cinv_hbm, map_hbm, mult_hbm, code_hbm, send_hbm,
    out_hbm,
    basis_ref, cinv_ref, map_ref, mult_ref, code_ref, send_ref, small_sem,
    load_v, a_v, s_v, load_sem, a_sem, s_sem, out_sem,
    bcol, brcol, brow, bslab, brecv, bs_sem, br_sem,
    mown, mrow, mtile, mall, ms_sem, mr_sem, zs_sem, zr_sem,
    onehot, twohot, selbuf, colz, colt, colall, cs_sem, cr_sem, ys_sem, yr_sem, wbuf,
    x, slab, rv0, rv1, rv2, rv3, rv4, rv5, rv6, rv7, es_sem, er_sem,
    sc, mul, res,
    pf, psend, prow, pall, ps_sem, pr_sem, qs_sem, qr_sem,
    cres, cin, cloc, cfar, cnear, ks_sem, kr_sem, ts_sem, tr_sem,
):
    nb, cases = load_v.shape
    nblk = nb // BLK
    cw = cases // CH
    rows = zs * ys * CORES
    rowdev = ys * CORES
    recv = (rv0, rv1, rv2, rv3, rv4, rv5, rv6, rv7)
    g = lax.axis_index("group")
    s = lax.axis_index("sub")
    c = lax.rem(s, CORES)
    zy = lax.div(s, CORES)
    y = lax.rem(zy, ys)
    z = lax.div(zy, ys)
    yc = y * CORES + c

    def sub_at(zz, yy, cc):
        return (zz * ys + yy) * CORES + cc

    def row_peer(dy, dc):
        yy = lax.rem(y + dy, ys)
        cc = lax.rem(c + dc, CORES)
        return (g, sub_at(z, yy, cc))

    def col_peer(dz):
        return (g, sub_at(lax.rem(z + dz, zs), y, c))

    def reader(d, core=None):
        at = s if core is None else sub_at(z, y, core)
        if d < 4:
            return (g, lax.rem(at + OFFSETS[d] + rows, rows))
        return (lax.rem(g + (1 if d == 4 else gs - 1), gs), at)

    row_steps = [(dy, dc) for dy in range(ys) for dc in range(CORES) if (dy, dc) != (0, 0)]
    col_steps = list(range(1, zs))
    started = []

    def remote(src, dst, ssem, rsem, dev):
        return pltpu.make_async_remote_copy(
            src_ref=src, dst_ref=dst, send_sem=ssem, recv_sem=rsem,
            device_id=dev, device_id_type=MESH,
        )

    barrier = pltpu.get_barrier_semaphore()
    peers = [row_peer(dy, dc) for dy, dc in row_steps]
    peers += [col_peer(dz) for dz in col_steps]
    first = sub_at(z, y, 0)
    for step in (-2, -1, 2, 3):
        peers.append((g, lax.rem(first + step + rows, rows)))
    for step in (1, gs - 1):
        for core in range(CORES):
            peers.append((lax.rem(g + step, gs), first + core))
    for peer in peers:
        pl.semaphore_signal(barrier, inc=1, device_id=peer, device_id_type=MESH)
    small = [
        pltpu.make_async_copy(src, dst, small_sem.at[n]) for n, (src, dst) in enumerate((
            (basis_hbm, basis_ref), (map_hbm, map_ref), (send_hbm, send_ref), (code_hbm, code_ref),
            (mult_hbm, mult_ref), (cinv_hbm, cinv_ref)))
    ]
    for copy in small:
        copy.start()
    load_copy = pltpu.make_async_copy(load_hbm.at[0, 0], load_v, load_sem)
    load_copy.start()
    tiles = nb // TILE

    def a_copy(t):
        part = pl.ds(t * TILE, TILE)
        return pltpu.make_async_copy(a_hbm.at[0, 0, part], a_v.at[part], a_sem.at[t])

    for t in range(tiles):
        a_copy(t).start()
    s_copy = pltpu.make_async_copy(s_hbm.at[0, 0], s_v, s_sem)
    s_copy.start()
    for copy in small:
        copy.wait()

    lane = lax.broadcasted_iota(jnp.int32, (8, 128), 1)
    mine = jnp.full((8, 128), -1, jnp.int32)
    for b in range(nblk):
        line = basis_ref[:, b * BLK:(b + 1) * BLK]
        brow[b:b + 1, :] = line
        bcol[b] = jnp.transpose(jnp.broadcast_to(line, (BLK, BLK)))
        mine = jnp.where(lane == b, b, mine)
        mine = jnp.where(lane == 64 + b, map_ref[0, b], mine)
    bslab[...] = jnp.zeros_like(bslab)
    for k in range(SLOTS):
        at = (k // CAP) * 8 + k % CAP
        block = jnp.maximum(send_ref[0, k], 0)
        mine = jnp.where(lane == PAD + at, block, mine)
        bslab[at:at + 1, :] = brow[pl.ds(block, 1), :]
    mown[...] = mine
    mrow[yc] = mine
    map_row = [
        remote(mown, mrow.at[yc], ms_sem.at[n], mr_sem.at[n], row_peer(dy, dc))
        for n, (dy, dc) in enumerate(row_steps)
    ]
    basis_out = [
        remote(bslab.at[pl.ds(d * 8, 8)], brecv.at[pl.ds(d * 8, 8)], bs_sem.at[d], br_sem.at[d], reader(d))
        for d in range(DIRS)
    ]
    started += map_row + basis_out

    def slab_copy(e, h, d):
        part = pl.ds(d * CAP, CAP)
        n = (e * CH + h) * DIRS + d
        return remote(
            slab.at[e * CH + h, part], recv[e * CH + h].at[part],
            es_sem.at[n], er_sem.at[n], reader(d),
        )

    def fill(e, h):
        for k in range(SLOTS):
            slab[e * CH + h, k] = x[h, jnp.maximum(send_ref[0, k], 0)]

    def send(e, h, dirs=ORDER):
        for d in dirs:
            copy = slab_copy(e, h, d)
            copy.start()
            started.append(copy)

    def wait_slabs(e, h):
        for d in ORDER:
            slab_copy(e, h, d).wait_recv()

    def p_fill(i, h):
        psend[i, h] = pf[h].astype(BF)

        @pl.when(c == h)
        def _():
            prow[i, yc] = pf[h].astype(BF)

    def p_send(i, h):
        dc = lax.rem(c + h, CORES)
        for dy in range(ys):
            n = (i * CH + h) * ys + dy
            copy = remote(
                psend.at[i, h], prow.at[i, yc], ps_sem.at[n],
                pr_sem.at[i * rowdev + dy * CORES + dc], row_peer(dy, dc),
            )
            if dy == 0:
                @pl.when(dc != 0)
                def _():
                    copy.start()
            else:
                copy.start()

    def p_wait_sends():
        for i in range(ITERS):
            for h in range(CH):
                dc = lax.rem(c + h, CORES)
                for dy in range(ys):
                    n = (i * CH + h) * ys + dy
                    copy = remote(
                        psend.at[i, h], prow.at[i, yc], ps_sem.at[n],
                        pr_sem.at[i * rowdev + dy * CORES + dc], row_peer(dy, dc),
                    )
                    if dy == 0:
                        @pl.when(dc != 0)
                        def _():
                            copy.wait_send()
                    else:
                        copy.wait_send()

    def q_copy(i, n, dz):
        return remote(
            prow.at[i], pall.at[i, z], qs_sem.at[i * zs + n], qr_sem.at[i * zs + n], col_peer(dz)
        )

    def relay(i):
        for dy, dc in row_steps:
            remote(
                psend.at[i, 0], prow.at[i, 0], ps_sem.at[0],
                pr_sem.at[i * rowdev + dy * CORES + dc], row_peer(dy, dc),
            ).wait_recv()
        for n, dz in enumerate(col_steps):
            q_copy(i, n, dz).start()
        pall[i, z] = prow[i]

    half = PAD + DIRS * 8

    def partner_copy(i):
        own = pl.ds((1 - c) * half, PAD)
        return remote(cres.at[i, own], cin.at[i], ks_sem.at[i], kr_sem.at[i], row_peer(0, 1))

    def far_copy(i, core, d):
        part = pl.ds(core * half + PAD + d * 8, 8)
        return remote(
            cres.at[i, part], cfar.at[i, c, pl.ds(d * 8, 8)],
            ts_sem.at[(i * CORES + core) * DIRS + d], tr_sem.at[(i * CH + c) * DIRS + d], reader(d, core),
        )

    def far_each(i, act):
        for d in range(DIRS):
            for core in range(CORES):
                if d == core:
                    @pl.when(c == core)
                    def _():
                        act(far_copy(i, core, d))
                else:
                    act(far_copy(i, core, d))

    def coarse(i):
        for n, dz in enumerate(col_steps):
            q_copy(i, n, dz).wait_recv()
        every = pall[i].reshape(rows * PAD, cw)
        cres[i] = jnp.dot(wbuf[...], every, preferred_element_type=F32)
        far_each(i, lambda copy: copy.start())
        partner_copy(i).start()
        for d in range(CORES):
            @pl.when(c != d)
            def _():
                cfar[i, c, d * 8:(d + 1) * 8, :] = cres[i, pl.ds(d * half + PAD + d * 8, 8), :]

    def collect(i, h):
        @pl.when(c == h)
        def _():
            cloc[h] = cres[i, pl.ds(h * half, PAD), :]

        @pl.when(c != h)
        def _():
            partner_copy(i).wait_recv()
            cloc[h] = cin[i]

        for d in range(DIRS):
            copy = remote(
                cres.at[i, pl.ds(0, 8)], cfar.at[i, h, pl.ds(d * 8, 8)],
                ts_sem.at[0], tr_sem.at[(i * CH + h) * DIRS + d], reader(d),
            )
            if d < CORES and d == 1 - h:
                @pl.when(c != h)
                def _():
                    copy.wait_recv()
            else:
                copy.wait_recv()
        cnear[h] = cfar[i, h]

    def code_row(b):
        code = code_ref[0, b]
        return code, (code // CAP) * 8 + code % CAP

    def weight(b):
        return 1.0 / jnp.full((1, 128), mult_ref[0, b].astype(F32))

    def keep(b, h, disp):
        pf[h, pl.ds(b, 1), :] = jnp.sum(bcol[b] * disp, axis=0, keepdims=True)
        x[h, b] = disp.astype(BF)

    per = TILE // BLK

    def first_solve():
        load_copy.wait()

        def step(t, carry):
            a_copy(t).wait()
            acc = jnp.dot(a_v[pl.ds(t * TILE, TILE), :], load_v[...], preferred_element_type=F32)
            for i in range(per):
                for h in range(CH):
                    keep(t * per + i, h, acc[i * BLK:(i + 1) * BLK, h * cw:(h + 1) * cw])
            return carry

        lax.fori_loop(0, tiles, step, 0)

    def solve(h):
        def step(t, carry):
            acc = jnp.dot(a_v[pl.ds(t * TILE, TILE), :], res[h], preferred_element_type=F32)
            for i in range(per):
                keep(t * per + i, h, acc[i * BLK:(i + 1) * BLK])
            return carry

        lax.fori_loop(0, tiles, step, 0)

    def scale(i, h):
        e = 2 * i
        wait_slabs(e, h)
        collect(i, h)

        def step(b, carry):
            code, at = code_row(b)
            own = x[h, b].astype(F32) + bcol[b] * cloc[h, pl.ds(b, 1), :]
            far = recv[e * CH + h][code].astype(F32) + brcol[b] * cnear[h, pl.ds(at, 1), :]
            sc[h, pl.ds(b * BLK, BLK), :] = ((own - far) * weight(b)).astype(BF)
            return carry

        lax.fori_loop(0, nblk, step, 0)

    def dirichlet(h):
        def step(t, carry):
            acc = jnp.dot(s_v[pl.ds(t * TILE, TILE), :], sc[h], preferred_element_type=F32)
            for i in range(per):
                b = t * per + i
                x[h, b] = (acc[i * BLK:(i + 1) * BLK] * weight(b)).astype(BF)
            return carry

        lax.fori_loop(0, tiles, step, 0)

    def update(i, h):
        e = 2 * i + 1
        wait_slabs(e, h)
        cols = slice(h * cw, (h + 1) * cw)

        def step(b, carry):
            part = pl.ds(b * BLK, BLK)
            new = x[h, b].astype(F32) - recv[e * CH + h][code_ref[0, b]].astype(F32)
            if i == 0:
                res[h, part, :] = (load_v[part, cols].astype(F32) - new).astype(BF)
            else:
                new = mul[part, cols] + new
            mul[part, cols] = new
            return carry

        lax.fori_loop(0, nblk, step, 0)

    def column_maps():
        for n in range(len(row_steps)):
            map_row[n].wait_recv()
        line = lax.broadcasted_iota(jnp.int32, (rowdev, 128), 0)
        tile = jnp.full((rowdev, 128), -1, jnp.int32)
        for n in range(rowdev):
            tile = jnp.where(line == n, mrow[n, 0:rowdev], tile)
        mtile[...] = tile
        copies = []
        for n, dz in enumerate(col_steps):
            copies.append(remote(mtile, mall.at[z], zs_sem.at[n], zr_sem.at[n], col_peer(dz)))
            copies[-1].start()
        mall[z] = tile
        started.extend(copies)
        return copies

    shift_row = (rowdev * PAD).bit_length() - 1
    shift_pad = PAD.bit_length() - 1

    def mark(dst, dofs):
        grid = jnp.transpose(dofs.astype(F32))[64:64 + PAD]
        width = dst.shape[1]
        ids = lax.broadcasted_iota(jnp.int32, (PAD, width), 1).astype(F32)
        for n in range(rows):
            hit = jnp.broadcast_to(grid[:, n:n + 1], (PAD, width)) == ids
            dst[n * PAD:(n + 1) * PAD, :] = jnp.where(hit, 1.0, 0.0).astype(BF)

    def columns(copies):
        for copy in copies:
            copy.wait_recv()
        mark(onehot, mall[...].reshape(rows, 128))
        picked = lax.dot_general(
            cinv_ref[0].astype(BF), onehot[...], (((1,), (1,)), ((), ())), preferred_element_type=F32
        ).astype(BF)
        lanes = rowdev * PAD
        copies = []
        for zz in range(zs):
            selbuf[zz] = picked[:, zz * lanes:(zz + 1) * lanes]
        for n, dz in enumerate(col_steps):
            zz = lax.rem(z + dz, zs)
            copies.append(remote(selbuf.at[zz], colz.at[z], cs_sem.at[n], cr_sem.at[n], col_peer(dz)))
            copies[-1].start()
        colz[z] = selbuf[z]
        started.extend(copies)
        return copies

    def mark_rows():
        dofs = mall[...].reshape(rows, 128)
        high = lax.shift_right_logical(dofs, shift_row)
        mid = lax.shift_right_logical(dofs, shift_pad) & (rowdev - 1)
        moved = mid * (zs * PAD) + high * PAD + (dofs & (PAD - 1))
        mark(twohot, jnp.where(dofs >= 0, moved, -1))

    def share_columns(copies):
        for copy in copies:
            copy.wait_recv()
        turned = jnp.transpose(colz[...].reshape(zs * PAD, rowdev * PAD).astype(F32)).astype(BF)
        colt[...] = turned.reshape(ys, CORES * PAD, zs * PAD)
        out = []
        for n, (dy, dc) in enumerate(row_steps):
            out.append(remote(
                colt.at[lax.rem(y + dy, ys)], colall.at[yc], ys_sem.at[n], yr_sem.at[n], row_peer(dy, dc)
            ))
            out[-1].start()
        colall[yc] = colt[y]
        started.extend(out)
        return out

    def coarse_rows(copies):
        width = CORES * PAD
        ids = lax.broadcasted_iota(jnp.int32, (half, width), 1).astype(F32)
        parts = []
        for core in range(CORES):
            table = jnp.broadcast_to(mrow[y * CORES + core, 0:1].astype(F32), (128, 128))
            want = jnp.transpose(table)[:half, :width]
            want = jnp.where(want >= 0, want + core * PAD, -1.0)
            parts.append(jnp.where(want == ids, 1.0, 0.0))
        wanted = jnp.concatenate(parts, axis=0).astype(BF)
        for copy in copies:
            copy.wait_recv()
        mat = jnp.concatenate([colall[n] for n in range(rowdev)], axis=1)
        both = lax.dot_general(
            mat, twohot[...], (((1,), (1,)), ((), ())), preferred_element_type=F32
        ).astype(BF)
        wbuf[...] = jnp.dot(wanted, both, preferred_element_type=F32).astype(BF)

    pf[...] = jnp.zeros_like(pf)
    first_solve()
    for h in range(CH):
        p_fill(0, h)
        fill(0, h)
    pl.semaphore_wait(barrier, len(peers))
    for copy in map_row:
        copy.start()
    for h in range(CH):
        p_send(0, h)
    for copy in basis_out:
        copy.start()
    for h in range(CH):
        send(0, h, ACROSS)
    map_col = column_maps()
    relay(0)
    send(0, 0, ALONG)
    col_out = columns(map_col)
    mark_rows()
    for copy in basis_out:
        copy.wait_recv()
    for b in range(nblk):
        _, at = code_row(b)
        brcol[b] = jnp.transpose(jnp.broadcast_to(brecv[pl.ds(at, 1), :], (BLK, BLK)))
    row_out = share_columns(col_out)
    send(0, 1, ALONG)
    coarse_rows(row_out)
    coarse(0)
    s_copy.wait()
    for h in range(CH):
        scale(0, h)
        dirichlet(h)
        fill(1, h)
        send(1, h)
    for h in range(CH):
        update(0, h)
        solve(h)
        p_fill(1, h)
        p_send(1, h)
        fill(2, h)
        send(2, h, ACROSS)

        @pl.when(c == h)
        def _():
            relay(1)

        send(2, h, ALONG)

    for h in range(CH):
        @pl.when(c == h)
        def _():
            coarse(1)

        scale(1, h)
        dirichlet(h)
        fill(3, h)
        send(3, h)
    outs = []
    for h in range(CH):
        update(1, h)
        cols = pl.ds(h * cw, cw)
        outs.append(pltpu.make_async_copy(mul.at[:, cols], out_hbm.at[0, 0, :, cols], out_sem.at[h]))
        outs[-1].start()

    for copy in started:
        copy.wait_send()
    p_wait_sends()
    for i in range(ITERS):
        for n, dz in enumerate(col_steps):
            q_copy(i, n, dz).wait_send()
        partner_copy(i).wait_send()
        far_each(i, lambda copy: copy.wait_send())
    for copy in outs:
        copy.wait()


def on_device(zs, ys, gs, *args):
    (load_cases, inv_schur, schur_blocks, coarse_basis, coarse_map,
     multiplicity, recv_code, send_blocks, coarse_inv) = args
    _, _, nb, cases = load_cases.shape
    nblk = nb // BLK
    cw = cases // CH
    own, nc = coarse_inv.shape[1:]
    rowdev = ys * CORES
    rows = zs * rowdev
    tiles = nb // TILE
    dma = pltpu.SemaphoreType.DMA
    vm = pltpu.VMEM
    exchanges = 2 * ITERS * CH
    half = PAD + DIRS * 8
    sm = pltpu.SMEM
    scratch = [
        vm((1, nb), F32), vm((1, own, nc), F32), sm((1, nblk), jnp.int32), sm((1, nblk), jnp.int32),
        sm((1, nblk), jnp.int32), sm((1, SLOTS), jnp.int32), dma((6,)),
        vm((nb, cases), BF), vm((nb, nb), BF), vm((nb, nb), BF),
        dma, dma((tiles,)), dma, dma((CH,)),
        vm((nblk, BLK, BLK), F32), vm((nblk, BLK, BLK), F32), vm((PAD, BLK), F32),
        vm((DIRS * 8, BLK), F32), vm((DIRS * 8, BLK), F32), dma((DIRS,)), dma((DIRS,)),
        vm((8, 128), jnp.int32), vm((rowdev, 8, 128), jnp.int32), vm((rowdev, 128), jnp.int32),
        vm((zs, rowdev, 128), jnp.int32), dma((rowdev,)), dma((rowdev,)), dma((zs,)), dma((zs,)),
        vm((rows * PAD, nc), BF), vm((rows * PAD, nc), BF),
        vm((zs, own, rowdev * PAD), BF), vm((zs, own, rowdev * PAD), BF),
        vm((ys, CORES * PAD, zs * own), BF), vm((rowdev, CORES * PAD, zs * own), BF),
        dma((zs,)), dma((zs,)), dma((rowdev,)), dma((rowdev,)), vm((CORES * half, rows * PAD), BF),
        vm((CH, nblk, BLK, cw), BF), vm((exchanges, SLOTS, BLK, cw), BF),
        *[vm((SLOTS, BLK, cw), BF) for _ in range(exchanges)],
        dma((exchanges * DIRS,)), dma((exchanges * DIRS,)),
        vm((CH, nb, cw), BF), vm((nb, cases), F32), vm((CH, nb, cw), BF),
        vm((CH, PAD, cw), F32), vm((ITERS, CH, PAD, cw), BF), vm((ITERS, rowdev, PAD, cw), BF),
        vm((ITERS, zs, rowdev, PAD, cw), BF),
        dma((ITERS * CH * ys,)), dma((ITERS * rowdev,)), dma((ITERS * zs,)), dma((ITERS * zs,)),
        vm((ITERS, CORES * half, cw), F32), vm((ITERS, PAD, cw), F32), vm((CH, PAD, cw), F32),
        vm((ITERS, CH, DIRS * 8, cw), F32), vm((CH, DIRS * 8, cw), F32), dma((ITERS,)), dma((ITERS,)),
        dma((ITERS * CORES * DIRS,)), dma((ITERS * CH * DIRS,)),
    ]
    hbm = pl.BlockSpec(memory_space=pl.ANY)
    return pl.pallas_call(
        functools.partial(kernel, zs, ys, gs),
        out_shape=jax.ShapeDtypeStruct(load_cases.shape, F32),
        in_specs=[hbm] * 9,
        out_specs=hbm,
        scratch_shapes=scratch,
        compiler_params=pltpu.CompilerParams(
            collective_id=0, has_side_effects=True, vmem_limit_bytes=60 * 1024 * 1024
        ),
        name="feti",
    )(
        load_cases, inv_schur, schur_blocks, coarse_basis[0], coarse_inv,
        coarse_map[0], multiplicity[0], recv_code[0], send_blocks[0],
    )


def build(mesh, zs, ys):
    wide = P("group", "sub", None, None)
    thin = P("group", "sub", None)
    return jax.shard_map(
        functools.partial(on_device, zs, ys, mesh.shape["group"]),
        mesh=mesh,
        in_specs=(wide, wide, wide, thin, thin, thin, thin, thin, thin),
        out_specs=wide,
        check_vma=False,
    )


def solution(mesh):
    ys = 4
    return build(mesh, mesh.shape["sub"] // (ys * CORES), ys)
```

```python
import functools

import jax
import jax.numpy as jnp
from jax import lax
from jax.experimental import pallas as pl
from jax.experimental.pallas import tpu as pltpu
from jax.sharding import PartitionSpec as P

BLK = 128
DIRS = 6
CAP = 4
ITERS = 2
SLOTS = DIRS * CAP
PAD = 16
CH = 2
CORES = 2
TILE = 256
OFFSETS = (1, -1, 2, -2)
ALONG = (2, 3, 0, 1)
ACROSS = (4, 5)
ORDER = ALONG + ACROSS
MESH = pl.DeviceIdType.MESH
BF = jnp.bfloat16
F32 = jnp.float32


def kernel(
    zs, ys, gs,
    load_hbm, a_hbm, s_hbm, basis_hbm, cinv_hbm, map_hbm, mult_hbm, code_hbm, send_hbm,
    out_hbm,
    basis_ref, cinv_ref, map_ref, mult_ref, code_ref, send_ref, small_sem,
    load_v, a_v, s_v, load_sem, a_sem, s_sem, out_sem,
    bcol, brcol, brow, bslab, brecv, bs_sem, br_sem,
    mown, mrow, mtile, mall, ms_sem, mr_sem, zs_sem, zr_sem,
    onehot, twohot, selbuf, colz, colt, colall, cs_sem, cr_sem, ys_sem, yr_sem, wbuf,
    x, slab, rv0, rv1, rv2, rv3, rv4, rv5, rv6, rv7, es_sem, er_sem,
    sc, mul, res,
    pf, psend, prow, pall, ps_sem, pr_sem, qs_sem, qr_sem,
    cres, cin, cloc, cfar, cnear, ks_sem, kr_sem, ts_sem, tr_sem,
):
    nb, cases = load_v.shape
    nblk = nb // BLK
    cw = cases // CH
    rows = zs * ys * CORES
    rowdev = ys * CORES
    recv = (rv0, rv1, rv2, rv3, rv4, rv5, rv6, rv7)
    g = lax.axis_index("group")
    s = lax.axis_index("sub")
    c = lax.rem(s, CORES)
    zy = lax.div(s, CORES)
    y = lax.rem(zy, ys)
    z = lax.div(zy, ys)
    yc = y * CORES + c

    def sub_at(zz, yy, cc):
        return (zz * ys + yy) * CORES + cc

    row_ids = [[(g, sub_at(z, lax.rem(y + dy, ys), cc)) for cc in (c, 1 - c)] for dy in range(ys)]
    col_ids = [(g, sub_at(lax.rem(z + dz, zs), y, c)) for dz in range(zs)]
    near = {step: lax.rem(s - c + step + rows, rows) for step in (-2, -1, 0, 1, 2, 3)}
    sides = [lax.rem(g + step, gs) for step in (1, gs - 1)]

    def reader_of(at, core, d):
        return (g, at(core + OFFSETS[d])) if d < 4 else (sides[d - 4], at(core))

    core_readers = [[reader_of(lambda step: near[step], core, d) for d in range(DIRS)] for core in range(CORES)]
    own_readers = [
        (jnp.where(c == 0, a[0], b[0]), jnp.where(c == 0, a[1], b[1])) for a, b in zip(*core_readers)
    ]

    def row_peer(dy, dc):
        if isinstance(dc, int):
            return row_ids[dy][dc]
        here, there = row_ids[dy]
        return (g, jnp.where(dc == 0, here[1], there[1]))

    def col_peer(dz):
        return col_ids[dz]

    def reader(d, core=None):
        return own_readers[d] if core is None else core_readers[core][d]

    row_steps = [(dy, dc) for dy in range(ys) for dc in range(CORES) if (dy, dc) != (0, 0)]
    col_steps = list(range(1, zs))
    started = []

    def remote(src, dst, ssem, rsem, dev):
        return pltpu.make_async_remote_copy(
            src_ref=src, dst_ref=dst, send_sem=ssem, recv_sem=rsem,
            device_id=dev, device_id_type=MESH,
        )

    barrier = pltpu.get_barrier_semaphore()
    peers = [row_peer(dy, dc) for dy, dc in row_steps]
    peers += [col_peer(dz) for dz in col_steps]
    peers += [(g, near[step]) for step in (-2, -1, 2, 3)]
    peers += [(side, near[core]) for side in sides for core in range(CORES)]
    for peer in peers:
        pl.semaphore_signal(barrier, inc=1, device_id=peer, device_id_type=MESH)
    small = [
        pltpu.make_async_copy(src, dst, small_sem.at[n]) for n, (src, dst) in enumerate((
            (basis_hbm, basis_ref), (map_hbm, map_ref), (send_hbm, send_ref), (code_hbm, code_ref),
            (mult_hbm, mult_ref), (cinv_hbm, cinv_ref)))
    ]
    for copy in small:
        copy.start()
    load_copy = pltpu.make_async_copy(load_hbm.at[0, 0], load_v, load_sem)
    load_copy.start()
    tiles = nb // TILE

    def a_copy(t):
        part = pl.ds(t * TILE, TILE)
        return pltpu.make_async_copy(a_hbm.at[0, 0, part], a_v.at[part], a_sem.at[t])

    for t in range(tiles):
        a_copy(t).start()
    s_copy = pltpu.make_async_copy(s_hbm.at[0, 0], s_v, s_sem)
    s_copy.start()
    for copy in small:
        copy.wait()

    lane = lax.broadcasted_iota(jnp.int32, (8, 128), 1)
    mine = jnp.full((8, 128), -1, jnp.int32)
    for b in range(nblk):
        line = basis_ref[:, b * BLK:(b + 1) * BLK]
        brow[b:b + 1, :] = line
        bcol[b] = jnp.transpose(jnp.broadcast_to(line, (BLK, BLK)))
        mine = jnp.where(lane == b, b, mine)
        mine = jnp.where(lane == 64 + b, map_ref[0, b], mine)
    bslab[...] = jnp.zeros_like(bslab)
    for k in range(SLOTS):
        at = (k // CAP) * 8 + k % CAP
        block = jnp.maximum(send_ref[0, k], 0)
        mine = jnp.where(lane == PAD + at, block, mine)
        bslab[at:at + 1, :] = brow[pl.ds(block, 1), :]
    mown[...] = mine
    mrow[yc] = mine
    map_row = [
        remote(mown, mrow.at[yc], ms_sem.at[n], mr_sem.at[n], row_peer(dy, dc))
        for n, (dy, dc) in enumerate(row_steps)
    ]
    basis_out = [
        remote(bslab.at[pl.ds(d * 8, 8)], brecv.at[pl.ds(d * 8, 8)], bs_sem.at[d], br_sem.at[d], reader(d))
        for d in range(DIRS)
    ]
    started += map_row + basis_out

    def slab_copy(e, h, d):
        part = pl.ds(d * CAP, CAP)
        n = (e * CH + h) * DIRS + d
        return remote(
            slab.at[e * CH + h, part], recv[e * CH + h].at[part],
            es_sem.at[n], er_sem.at[n], reader(d),
        )

    def fill(e, h):
        for k in range(SLOTS):
            slab[e * CH + h, k] = x[h, jnp.maximum(send_ref[0, k], 0)]

    def send(e, h, dirs=ORDER):
        for d in dirs:
            copy = slab_copy(e, h, d)
            copy.start()
            started.append(copy)

    def wait_slabs(e, h):
        for d in ORDER:
            slab_copy(e, h, d).wait_recv()

    def p_fill(i, h):
        psend[i, h] = pf[h].astype(BF)

        @pl.when(c == h)
        def _():
            prow[i, yc] = pf[h].astype(BF)

    def p_send(i, h):
        dc = lax.rem(c + h, CORES)
        for dy in range(ys):
            n = (i * CH + h) * ys + dy
            copy = remote(
                psend.at[i, h], prow.at[i, yc], ps_sem.at[n],
                pr_sem.at[i * rowdev + dy * CORES + dc], row_peer(dy, dc),
            )
            if dy == 0:
                @pl.when(dc != 0)
                def _():
                    copy.start()
            else:
                copy.start()

    def p_wait_sends():
        for i in range(ITERS):
            for h in range(CH):
                dc = lax.rem(c + h, CORES)
                for dy in range(ys):
                    n = (i * CH + h) * ys + dy
                    copy = remote(
                        psend.at[i, h], prow.at[i, yc], ps_sem.at[n],
                        pr_sem.at[i * rowdev + dy * CORES + dc], row_peer(dy, dc),
                    )
                    if dy == 0:
                        @pl.when(dc != 0)
                        def _():
                            copy.wait_send()
                    else:
                        copy.wait_send()

    def q_copy(i, n, dz):
        return remote(
            prow.at[i], pall.at[i, z], qs_sem.at[i * zs + n], qr_sem.at[i * zs + n], col_peer(dz)
        )

    def relay(i):
        for dy, dc in row_steps:
            remote(
                psend.at[i, 0], prow.at[i, 0], ps_sem.at[0],
                pr_sem.at[i * rowdev + dy * CORES + dc], row_peer(dy, dc),
            ).wait_recv()
        for n, dz in enumerate(col_steps):
            q_copy(i, n, dz).start()
        pall[i, z] = prow[i]

    half = PAD + DIRS * 8

    def partner_copy(i):
        own = pl.ds((1 - c) * half, PAD)
        return remote(cres.at[i, own], cin.at[i], ks_sem.at[i], kr_sem.at[i], row_peer(0, 1))

    def far_copy(i, core, d):
        part = pl.ds(core * half + PAD + d * 8, 8)
        return remote(
            cres.at[i, part], cfar.at[i, c, pl.ds(d * 8, 8)],
            ts_sem.at[(i * CORES + core) * DIRS + d], tr_sem.at[(i * CH + c) * DIRS + d], reader(d, core),
        )

    def far_each(i, act):
        for d in range(DIRS):
            for core in range(CORES):
                if d == core:
                    @pl.when(c == core)
                    def _():
                        act(far_copy(i, core, d))
                else:
                    act(far_copy(i, core, d))

    def coarse(i):
        for n, dz in enumerate(col_steps):
            q_copy(i, n, dz).wait_recv()
        every = pall[i].reshape(rows * PAD, cw)
        cres[i] = jnp.dot(wbuf[...], every, preferred_element_type=F32)
        far_each(i, lambda copy: copy.start())
        partner_copy(i).start()
        for d in range(CORES):
            @pl.when(c != d)
            def _():
                cfar[i, c, d * 8:(d + 1) * 8, :] = cres[i, pl.ds(d * half + PAD + d * 8, 8), :]

    def collect(i, h):
        @pl.when(c == h)
        def _():
            cloc[h] = cres[i, pl.ds(h * half, PAD), :]

        @pl.when(c != h)
        def _():
            partner_copy(i).wait_recv()
            cloc[h] = cin[i]

        for d in range(DIRS):
            copy = remote(
                cres.at[i, pl.ds(0, 8)], cfar.at[i, h, pl.ds(d * 8, 8)],
                ts_sem.at[0], tr_sem.at[(i * CH + h) * DIRS + d], reader(d),
            )
            if d < CORES and d == 1 - h:
                @pl.when(c != h)
                def _():
                    copy.wait_recv()
            else:
                copy.wait_recv()
        cnear[h] = cfar[i, h]

    def code_row(b):
        code = code_ref[0, b]
        return code, (code // CAP) * 8 + code % CAP

    def weight(b):
        return 1.0 / jnp.full((1, 128), mult_ref[0, b].astype(F32))

    def keep(b, h, disp):
        pf[h, pl.ds(b, 1), :] = jnp.sum(bcol[b] * disp, axis=0, keepdims=True)
        x[h, b] = disp.astype(BF)

    per = TILE // BLK

    def first_solve():
        load_copy.wait()

        def step(t, carry):
            a_copy(t).wait()
            acc = jnp.dot(a_v[pl.ds(t * TILE, TILE), :], load_v[...], preferred_element_type=F32)
            for i in range(per):
                for h in range(CH):
                    keep(t * per + i, h, acc[i * BLK:(i + 1) * BLK, h * cw:(h + 1) * cw])
            return carry

        lax.fori_loop(0, tiles, step, 0)

    def solve(h):
        acc = jnp.dot(a_v[...], res[h], preferred_element_type=F32)
        for b in range(nblk):
            keep(b, h, acc[b * BLK:(b + 1) * BLK])

    def scale(i, h):
        e = 2 * i
        wait_slabs(e, h)
        collect(i, h)

        def step(b, carry):
            code, at = code_row(b)
            own = x[h, b].astype(F32) + bcol[b] * cloc[h, pl.ds(b, 1), :]
            far = recv[e * CH + h][code].astype(F32) + brcol[b] * cnear[h, pl.ds(at, 1), :]
            sc[h, pl.ds(b * BLK, BLK), :] = ((own - far) * weight(b)).astype(BF)
            return carry

        lax.fori_loop(0, nblk, step, 0)

    def dirichlet(h):
        acc = jnp.dot(s_v[...], sc[h], preferred_element_type=F32)
        for b in range(nblk):
            x[h, b] = (acc[b * BLK:(b + 1) * BLK] * weight(b)).astype(BF)

    def update(i, h):
        e = 2 * i + 1
        wait_slabs(e, h)
        cols = slice(h * cw, (h + 1) * cw)

        def step(b, carry):
            part = pl.ds(b * BLK, BLK)
            new = x[h, b].astype(F32) - recv[e * CH + h][code_ref[0, b]].astype(F32)
            if i == 0:
                res[h, part, :] = (load_v[part, cols].astype(F32) - new).astype(BF)
            else:
                new = mul[part, cols] + new
            mul[part, cols] = new
            return carry

        lax.fori_loop(0, nblk, step, 0)

    def column_maps():
        for n in range(len(row_steps)):
            map_row[n].wait_recv()
        line = lax.broadcasted_iota(jnp.int32, (rowdev, 128), 0)
        tile = jnp.full((rowdev, 128), -1, jnp.int32)
        for n in range(rowdev):
            tile = jnp.where(line == n, mrow[n, 0:rowdev], tile)
        mtile[...] = tile
        copies = []
        for n, dz in enumerate(col_steps):
            copies.append(remote(mtile, mall.at[z], zs_sem.at[n], zr_sem.at[n], col_peer(dz)))
            copies[-1].start()
        mall[z] = tile
        started.extend(copies)
        return copies

    shift_row = (rowdev * PAD).bit_length() - 1
    shift_pad = PAD.bit_length() - 1

    def mark(dst, dofs):
        grid = jnp.transpose(dofs.astype(F32))[64:64 + PAD]
        width = dst.shape[1]
        ids = lax.broadcasted_iota(jnp.int32, (PAD, width), 1).astype(F32)
        for n in range(rows):
            hit = jnp.broadcast_to(grid[:, n:n + 1], (PAD, width)) == ids
            dst[n * PAD:(n + 1) * PAD, :] = jnp.where(hit, 1.0, 0.0).astype(BF)

    def columns(copies):
        for copy in copies:
            copy.wait_recv()
        mark(onehot, mall[...].reshape(rows, 128))
        picked = lax.dot_general(
            cinv_ref[0].astype(BF), onehot[...], (((1,), (1,)), ((), ())), preferred_element_type=F32
        ).astype(BF)
        lanes = rowdev * PAD
        copies = []
        for zz in range(zs):
            selbuf[zz] = picked[:, zz * lanes:(zz + 1) * lanes]
        for n, dz in enumerate(col_steps):
            zz = lax.rem(z + dz, zs)
            copies.append(remote(selbuf.at[zz], colz.at[z], cs_sem.at[n], cr_sem.at[n], col_peer(dz)))
            copies[-1].start()
        colz[z] = selbuf[z]
        started.extend(copies)
        return copies

    def mark_rows():
        dofs = mall[...].reshape(rows, 128)
        high = lax.shift_right_logical(dofs, shift_row)
        mid = lax.shift_right_logical(dofs, shift_pad) & (rowdev - 1)
        moved = mid * (zs * PAD) + high * PAD + (dofs & (PAD - 1))
        mark(twohot, jnp.where(dofs >= 0, moved, -1))

    def share_columns(copies):
        for copy in copies:
            copy.wait_recv()
        turned = jnp.transpose(colz[...].reshape(zs * PAD, rowdev * PAD).astype(F32)).astype(BF)
        colt[...] = turned.reshape(ys, CORES * PAD, zs * PAD)
        out = []
        for n, (dy, dc) in enumerate(row_steps):
            out.append(remote(
                colt.at[lax.rem(y + dy, ys)], colall.at[yc], ys_sem.at[n], yr_sem.at[n], row_peer(dy, dc)
            ))
            out[-1].start()
        colall[yc] = colt[y]
        started.extend(out)
        return out

    def coarse_rows(copies):
        width = CORES * PAD
        ids = lax.broadcasted_iota(jnp.int32, (half, width), 1).astype(F32)
        parts = []
        for core in range(CORES):
            table = jnp.broadcast_to(mrow[y * CORES + core, 0:1].astype(F32), (128, 128))
            want = jnp.transpose(table)[:half, :width]
            want = jnp.where(want >= 0, want + core * PAD, -1.0)
            parts.append(jnp.where(want == ids, 1.0, 0.0))
        wanted = jnp.concatenate(parts, axis=0).astype(BF)
        for copy in copies:
            copy.wait_recv()
        mat = jnp.concatenate([colall[n] for n in range(rowdev)], axis=1)
        both = lax.dot_general(
            mat, twohot[...], (((1,), (1,)), ((), ())), preferred_element_type=F32
        ).astype(BF)
        wbuf[...] = jnp.dot(wanted, both, preferred_element_type=F32).astype(BF)

    pf[...] = jnp.zeros_like(pf)
    first_solve()
    for h in range(CH):
        p_fill(0, h)
        fill(0, h)
    pl.semaphore_wait(barrier, len(peers))
    for copy in map_row:
        copy.start()
    for h in range(CH):
        p_send(0, h)
    for copy in basis_out:
        copy.start()
    for h in range(CH):
        send(0, h)
    map_col = column_maps()
    col_out = columns(map_col)
    relay(0)
    mark_rows()
    for copy in basis_out:
        copy.wait_recv()
    for b in range(nblk):
        _, at = code_row(b)
        brcol[b] = jnp.transpose(jnp.broadcast_to(brecv[pl.ds(at, 1), :], (BLK, BLK)))
    row_out = share_columns(col_out)
    coarse_rows(row_out)
    coarse(0)
    s_copy.wait()
    for h in range(CH):
        scale(0, h)
        dirichlet(h)
        fill(1, h)
        send(1, h)
    for h in range(CH):
        update(0, h)
        solve(h)
        p_fill(1, h)
        p_send(1, h)
        fill(2, h)
        send(2, h)

        @pl.when(c == h)
        def _():
            relay(1)

    for h in range(CH):
        @pl.when(c == h)
        def _():
            coarse(1)

        scale(1, h)
        dirichlet(h)
        fill(3, h)
        send(3, h)
    outs = []
    for h in range(CH):
        update(1, h)
        cols = pl.ds(h * cw, cw)
        outs.append(pltpu.make_async_copy(mul.at[:, cols], out_hbm.at[0, 0, :, cols], out_sem.at[h]))
        outs[-1].start()

    for copy in started:
        copy.wait_send()
    p_wait_sends()
    for i in range(ITERS):
        for n, dz in enumerate(col_steps):
            q_copy(i, n, dz).wait_send()
        partner_copy(i).wait_send()
        far_each(i, lambda copy: copy.wait_send())
    for copy in outs:
        copy.wait()


def on_device(zs, ys, gs, *args):
    (load_cases, inv_schur, schur_blocks, coarse_basis, coarse_map,
     multiplicity, recv_code, send_blocks, coarse_inv) = args
    _, _, nb, cases = load_cases.shape
    nblk = nb // BLK
    cw = cases // CH
    own, nc = coarse_inv.shape[1:]
    rowdev = ys * CORES
    rows = zs * rowdev
    tiles = nb // TILE
    dma = pltpu.SemaphoreType.DMA
    vm = pltpu.VMEM
    exchanges = 2 * ITERS * CH
    half = PAD + DIRS * 8
    sm = pltpu.SMEM
    scratch = [
        vm((1, nb), F32), vm((1, own, nc), F32), sm((1, nblk), jnp.int32), sm((1, nblk), jnp.int32),
        sm((1, nblk), jnp.int32), sm((1, SLOTS), jnp.int32), dma((6,)),
        vm((nb, cases), BF), vm((nb, nb), BF), vm((nb, nb), BF),
        dma, dma((tiles,)), dma, dma((CH,)),
        vm((nblk, BLK, BLK), F32), vm((nblk, BLK, BLK), F32), vm((PAD, BLK), F32),
        vm((DIRS * 8, BLK), F32), vm((DIRS * 8, BLK), F32), dma((DIRS,)), dma((DIRS,)),
        vm((8, 128), jnp.int32), vm((rowdev, 8, 128), jnp.int32), vm((rowdev, 128), jnp.int32),
        vm((zs, rowdev, 128), jnp.int32), dma((rowdev,)), dma((rowdev,)), dma((zs,)), dma((zs,)),
        vm((rows * PAD, nc), BF), vm((rows * PAD, nc), BF),
        vm((zs, own, rowdev * PAD), BF), vm((zs, own, rowdev * PAD), BF),
        vm((ys, CORES * PAD, zs * own), BF), vm((rowdev, CORES * PAD, zs * own), BF),
        dma((zs,)), dma((zs,)), dma((rowdev,)), dma((rowdev,)), vm((CORES * half, rows * PAD), BF),
        vm((CH, nblk, BLK, cw), BF), vm((exchanges, SLOTS, BLK, cw), BF),
        *[vm((SLOTS, BLK, cw), BF) for _ in range(exchanges)],
        dma((exchanges * DIRS,)), dma((exchanges * DIRS,)),
        vm((CH, nb, cw), BF), vm((nb, cases), F32), vm((CH, nb, cw), BF),
        vm((CH, PAD, cw), F32), vm((ITERS, CH, PAD, cw), BF), vm((ITERS, rowdev, PAD, cw), BF),
        vm((ITERS, zs, rowdev, PAD, cw), BF),
        dma((ITERS * CH * ys,)), dma((ITERS * rowdev,)), dma((ITERS * zs,)), dma((ITERS * zs,)),
        vm((ITERS, CORES * half, cw), F32), vm((ITERS, PAD, cw), F32), vm((CH, PAD, cw), F32),
        vm((ITERS, CH, DIRS * 8, cw), F32), vm((CH, DIRS * 8, cw), F32), dma((ITERS,)), dma((ITERS,)),
        dma((ITERS * CORES * DIRS,)), dma((ITERS * CH * DIRS,)),
    ]
    hbm = pl.BlockSpec(memory_space=pl.ANY)
    return pl.pallas_call(
        functools.partial(kernel, zs, ys, gs),
        out_shape=jax.ShapeDtypeStruct(load_cases.shape, F32),
        in_specs=[hbm] * 9,
        out_specs=hbm,
        scratch_shapes=scratch,
        compiler_params=pltpu.CompilerParams(
            collective_id=0, has_side_effects=True, vmem_limit_bytes=60 * 1024 * 1024
        ),
        name="feti",
    )(
        load_cases, inv_schur, schur_blocks, coarse_basis[0], coarse_inv,
        coarse_map[0], multiplicity[0], recv_code[0], send_blocks[0],
    )


def build(mesh, zs, ys):
    wide = P("group", "sub", None, None)
    thin = P("group", "sub", None)
    return jax.shard_map(
        functools.partial(on_device, zs, ys, mesh.shape["group"]),
        mesh=mesh,
        in_specs=(wide, wide, wide, thin, thin, thin, thin, thin, thin),
        out_specs=wide,
        check_vma=False,
    )


def solution(mesh):
    ys = 4
    return build(mesh, mesh.shape["sub"] // (ys * CORES), ys)
```

```python
import functools

import jax
import jax.numpy as jnp
from jax import lax
from jax.experimental import pallas as pl
from jax.experimental.pallas import tpu as pltpu
from jax.sharding import PartitionSpec as P

BLK = 128
DIRS = 6
CAP = 4
ITERS = 2
SLOTS = DIRS * CAP
PAD = 16
CH = 2
CORES = 2
TERMS = 2 * PAD
TILE = 256
OFFSETS = (1, -1, 2, -2)
ALONG = (2, 3, 0, 1)
ACROSS = (4, 5)
ORDER = ALONG + ACROSS
MESH = pl.DeviceIdType.MESH
BF = jnp.bfloat16
F32 = jnp.float32


def kernel(
    zs, ys, gs,
    load_hbm, a_hbm, s_hbm, basis_hbm, cinv_hbm, map_hbm, mult_hbm, code_hbm, send_hbm,
    out_hbm,
    basis_ref, cinv_ref, map_ref, mult_ref, code_ref, send_ref, small_sem,
    load_v, a_v, s_v, load_sem, a_sem, s_sem, out_sem,
    bcol, brow, bslab, brecv, bs_sem, br_sem,
    mown, mrow, mtile, mall, ms_sem, mr_sem, zs_sem, zr_sem,
    onehot, twohot, selbuf, colz, colt, colall, cs_sem, cr_sem, ys_sem, yr_sem, wbuf,
    x, slab, rv0, rv1, rv2, rv3, rv4, rv5, rv6, rv7, es_sem, er_sem,
    sc, mul, res,
    pf, psend, prow, pall, ps_sem, pr_sem, qs_sem, qr_sem,
    cres, cin, cloc, cfar, cnear, ks_sem, kr_sem, ts_sem, tr_sem,
    dmat, gt, gslab, grecv, gs_sem, gr_sem, gg, ccf, ccs, ccr, call, us_sem, ur_sem,
):
    nb, cases = load_v.shape
    nblk = nb // BLK
    cw = cases // CH
    rows = zs * ys * CORES
    rowdev = ys * CORES
    recv = (rv0, rv1, rv2, rv3, rv4, rv5, rv6, rv7)
    g = lax.axis_index("group")
    s = lax.axis_index("sub")
    c = lax.rem(s, CORES)
    zy = lax.div(s, CORES)
    y = lax.rem(zy, ys)
    z = lax.div(zy, ys)
    yc = y * CORES + c

    def sub_at(zz, yy, cc):
        return (zz * ys + yy) * CORES + cc

    row_ids = [[(g, sub_at(z, lax.rem(y + dy, ys), cc)) for cc in (c, 1 - c)] for dy in range(ys)]
    col_ids = [(g, sub_at(lax.rem(z + dz, zs), y, c)) for dz in range(zs)]
    near = {step: lax.rem(s - c + step + rows, rows) for step in (-2, -1, 0, 1, 2, 3)}
    sides = [lax.rem(g + step, gs) for step in (1, gs - 1)]

    def reader_of(at, core, d):
        return (g, at(core + OFFSETS[d])) if d < 4 else (sides[d - 4], at(core))

    core_readers = [[reader_of(lambda step: near[step], core, d) for d in range(DIRS)] for core in range(CORES)]
    own_readers = [
        (jnp.where(c == 0, a[0], b[0]), jnp.where(c == 0, a[1], b[1])) for a, b in zip(*core_readers)
    ]

    def row_peer(dy, dc):
        if isinstance(dc, int):
            return row_ids[dy][dc]
        here, there = row_ids[dy]
        return (g, jnp.where(dc == 0, here[1], there[1]))

    def col_peer(dz):
        return col_ids[dz]

    def reader(d, core=None):
        return own_readers[d] if core is None else core_readers[core][d]

    row_steps = [(dy, dc) for dy in range(ys) for dc in range(CORES) if (dy, dc) != (0, 0)]
    col_steps = list(range(1, zs))
    started = []

    def remote(src, dst, ssem, rsem, dev):
        return pltpu.make_async_remote_copy(
            src_ref=src, dst_ref=dst, send_sem=ssem, recv_sem=rsem,
            device_id=dev, device_id_type=MESH,
        )

    barrier = pltpu.get_barrier_semaphore()
    peers = [row_peer(dy, dc) for dy, dc in row_steps]
    peers += [col_peer(dz) for dz in col_steps]
    peers += [(g, near[step]) for step in (-2, -1, 2, 3)]
    peers += [(side, near[core]) for side in sides for core in range(CORES)]
    for peer in peers:
        pl.semaphore_signal(barrier, inc=1, device_id=peer, device_id_type=MESH)
    small = [
        pltpu.make_async_copy(src, dst, small_sem.at[n]) for n, (src, dst) in enumerate((
            (basis_hbm, basis_ref), (map_hbm, map_ref), (send_hbm, send_ref), (code_hbm, code_ref),
            (mult_hbm, mult_ref), (cinv_hbm, cinv_ref)))
    ]
    for copy in small:
        copy.start()
    load_copy = pltpu.make_async_copy(load_hbm.at[0, 0], load_v, load_sem)
    load_copy.start()
    tiles = nb // TILE

    def a_copy(t):
        part = pl.ds(t * TILE, TILE)
        return pltpu.make_async_copy(a_hbm.at[0, 0, part], a_v.at[part], a_sem.at[t])

    for t in range(tiles):
        a_copy(t).start()
    s_copy = pltpu.make_async_copy(s_hbm.at[0, 0], s_v, s_sem)
    s_copy.start()
    for copy in small:
        copy.wait()

    lane = lax.broadcasted_iota(jnp.int32, (8, 128), 1)
    mine = jnp.full((8, 128), -1, jnp.int32)
    for b in range(nblk):
        line = basis_ref[:, b * BLK:(b + 1) * BLK]
        brow[b:b + 1, :] = line
        bcol[b] = jnp.transpose(jnp.broadcast_to(line, (BLK, BLK)))
        mine = jnp.where(lane == b, b, mine)
        mine = jnp.where(lane == 64 + b, map_ref[0, b], mine)
    bslab[...] = jnp.zeros_like(bslab)
    for k in range(SLOTS):
        at = (k // CAP) * 8 + k % CAP
        block = jnp.maximum(send_ref[0, k], 0)
        mine = jnp.where(lane == PAD + at, block, mine)
        bslab[at:at + 1, :] = brow[pl.ds(block, 1), :]
    mown[...] = mine
    mrow[yc] = mine
    map_row = [
        remote(mown, mrow.at[yc], ms_sem.at[n], mr_sem.at[n], row_peer(dy, dc))
        for n, (dy, dc) in enumerate(row_steps)
    ]
    basis_out = [
        remote(bslab.at[pl.ds(d * 8, 8)], brecv.at[pl.ds(d * 8, 8)], bs_sem.at[d], br_sem.at[d], reader(d))
        for d in range(DIRS)
    ]
    started += map_row + basis_out

    def slab_copy(e, h, d):
        part = pl.ds(d * CAP, CAP)
        n = (e * CH + h) * DIRS + d
        return remote(
            slab.at[e * CH + h, part], recv[e * CH + h].at[part],
            es_sem.at[n], er_sem.at[n], reader(d),
        )

    def fill(e, h):
        for k in range(SLOTS):
            slab[e * CH + h, k] = x[h, jnp.maximum(send_ref[0, k], 0)]

    def send(e, h, dirs=ORDER):
        for d in dirs:
            copy = slab_copy(e, h, d)
            copy.start()
            started.append(copy)

    def wait_slabs(e, h):
        for d in ORDER:
            slab_copy(e, h, d).wait_recv()

    def p_fill(i, h):
        psend[i, h] = pf[h].astype(BF)

        @pl.when(c == h)
        def _():
            prow[i, yc] = pf[h].astype(BF)

    def p_send(i, h):
        dc = lax.rem(c + h, CORES)
        for dy in range(ys):
            n = (i * CH + h) * ys + dy
            copy = remote(
                psend.at[i, h], prow.at[i, yc], ps_sem.at[n],
                pr_sem.at[i * rowdev + dy * CORES + dc], row_peer(dy, dc),
            )
            if dy == 0:
                @pl.when(dc != 0)
                def _():
                    copy.start()
            else:
                copy.start()

    def p_wait_sends():
        for i in range(ITERS):
            for h in range(CH):
                dc = lax.rem(c + h, CORES)
                for dy in range(ys):
                    n = (i * CH + h) * ys + dy
                    copy = remote(
                        psend.at[i, h], prow.at[i, yc], ps_sem.at[n],
                        pr_sem.at[i * rowdev + dy * CORES + dc], row_peer(dy, dc),
                    )
                    if dy == 0:
                        @pl.when(dc != 0)
                        def _():
                            copy.wait_send()
                    else:
                        copy.wait_send()

    def q_copy(i, n, dz):
        return remote(
            prow.at[i], pall.at[i, z], qs_sem.at[i * zs + n], qr_sem.at[i * zs + n], col_peer(dz)
        )

    def relay(i):
        for dy, dc in row_steps:
            remote(
                psend.at[i, 0], prow.at[i, 0], ps_sem.at[0],
                pr_sem.at[i * rowdev + dy * CORES + dc], row_peer(dy, dc),
            ).wait_recv()
        for n, dz in enumerate(col_steps):
            q_copy(i, n, dz).start()
        pall[i, z] = prow[i]

    half = PAD + DIRS * 8

    def partner_copy(i):
        own = pl.ds((1 - c) * half, PAD)
        return remote(cres.at[i, own], cin.at[i], ks_sem.at[i], kr_sem.at[i], row_peer(0, 1))

    def far_copy(i, core, d):
        part = pl.ds(core * half + PAD + d * 8, 8)
        return remote(
            cres.at[i, part], cfar.at[i, c, pl.ds(d * 8, 8)],
            ts_sem.at[(i * CORES + core) * DIRS + d], tr_sem.at[(i * CH + c) * DIRS + d], reader(d, core),
        )

    def far_each(i, act):
        for d in range(DIRS):
            for core in range(CORES):
                if d == core:
                    @pl.when(c == core)
                    def _():
                        act(far_copy(i, core, d))
                else:
                    act(far_copy(i, core, d))

    def coarse(i):
        for n, dz in enumerate(col_steps):
            q_copy(i, n, dz).wait_recv()
        every = pall[i].reshape(rows * PAD, cw)
        cres[i] = jnp.dot(wbuf[...], every, preferred_element_type=F32)
        far_each(i, lambda copy: copy.start())
        partner_copy(i).start()
        for d in range(CORES):
            @pl.when(c != d)
            def _():
                cfar[i, c, d * 8:(d + 1) * 8, :] = cres[i, pl.ds(d * half + PAD + d * 8, 8), :]

    def collect(i, h):
        @pl.when(c == h)
        def _():
            cloc[h] = cres[i, pl.ds(h * half, PAD), :]

        @pl.when(c != h)
        def _():
            partner_copy(i).wait_recv()
            cloc[h] = cin[i]

        for d in range(DIRS):
            copy = remote(
                cres.at[i, pl.ds(0, 8)], cfar.at[i, h, pl.ds(d * 8, 8)],
                ts_sem.at[0], tr_sem.at[(i * CH + h) * DIRS + d], reader(d),
            )
            if d < CORES and d == 1 - h:
                @pl.when(c != h)
                def _():
                    copy.wait_recv()
            else:
                copy.wait_recv()
        cnear[h] = cfar[i, h]

    def code_row(b):
        code = code_ref[0, b]
        return code, (code // CAP) * 8 + code % CAP

    def weight(b):
        return 1.0 / jnp.full((1, 128), mult_ref[0, b].astype(F32))

    def keep(b, h, disp):
        pf[h, pl.ds(b, 1), :] = jnp.sum(bcol[b] * disp, axis=0, keepdims=True)
        x[h, b] = disp.astype(BF)

    per = TILE // BLK

    def first_solve():
        load_copy.wait()

        def step(t, carry):
            a_copy(t).wait()
            acc = jnp.dot(a_v[pl.ds(t * TILE, TILE), :], load_v[...], preferred_element_type=F32)
            for i in range(per):
                for h in range(CH):
                    keep(t * per + i, h, acc[i * BLK:(i + 1) * BLK, h * cw:(h + 1) * cw])
            return carry

        lax.fori_loop(0, tiles, step, 0)

    def solve(h):
        acc = jnp.dot(a_v[...], res[h], preferred_element_type=F32)
        for b in range(nblk):
            keep(b, h, acc[b * BLK:(b + 1) * BLK])

    def scale(i, h):
        e = 2 * i
        wait_slabs(e, h)

        def step(b, carry):
            code, _ = code_row(b)
            diff = x[h, b].astype(F32) - recv[e * CH + h][code].astype(F32)
            sc[h, pl.ds(b * BLK, BLK), :] = (diff * weight(b)).astype(BF)
            return carry

        lax.fori_loop(0, nblk, step, 0)

    def response():
        for copy in basis_out:
            copy.wait_recv()
        lanes = lax.broadcasted_iota(jnp.int32, (BLK, BLK), 1)
        for b in range(nblk):
            _, at = code_row(b)
            far = jnp.transpose(jnp.broadcast_to(brecv[pl.ds(at, 1), :], (BLK, BLK)))
            both = jnp.where(lanes == b, bcol[b], jnp.where(lanes == PAD + b, -far, 0.0))
            dmat[b * BLK:(b + 1) * BLK, :] = (both * weight(b)).astype(BF)
        s_copy.wait()
        acc = jnp.dot(s_v[...], dmat[...], preferred_element_type=F32)
        for b in range(nblk):
            turned = jnp.transpose(acc[b * BLK:(b + 1) * BLK] * weight(b))
            gt[b] = turned[:TERMS].astype(BF)
        for k in range(SLOTS):
            gslab[k] = gt[jnp.maximum(send_ref[0, k], 0)]
        copies = []
        for d in ORDER:
            part = pl.ds(d * CAP, CAP)
            copies.append(remote(gslab.at[part], grecv.at[part], gs_sem.at[d], gr_sem.at[d], reader(d)))
            copies[-1].start()
        started.extend(copies)
        return copies

    def responses(copies):
        for copy in copies:
            copy.wait_recv()
        rest = jnp.zeros((2 * BLK - (1 + DIRS) * TERMS, BLK), F32)
        for b in range(nblk):
            code, _ = code_row(b)
            far = -grecv[code].astype(F32)
            source = jnp.full(far.shape, code // CAP, jnp.int32)
            pieces = [gt[b].astype(F32)]
            pieces += [jnp.where(source == d, far, 0.0) for d in range(DIRS)] + [rest]
            wide = jnp.concatenate(pieces, axis=0)
            gg[b * BLK:(b + 1) * BLK, :BLK] = jnp.transpose(wide[:BLK]).astype(BF)
            gg[b * BLK:(b + 1) * BLK, BLK:] = jnp.transpose(wide[BLK:]).astype(BF)

    def cc_copy(i, h, d):
        n = i * CH + h
        return remote(
            ccs.at[n], ccr.at[n, d], us_sem.at[n * DIRS + d], ur_sem.at[n * DIRS + d], reader(d)
        )

    def cc_send(i, h):
        collect(i, h)
        ccf[...] = jnp.zeros_like(ccf)
        ccf[0:PAD, :] = cloc[h]
        for b in range(nblk):
            _, at = code_row(b)
            ccf[PAD + b:PAD + b + 1, :] = cnear[h, pl.ds(at, 1), :]
        ccs[i * CH + h] = ccf[...].astype(BF)
        for d in ORDER:
            copy = cc_copy(i, h, d)
            copy.start()
            started.append(copy)

    def dirichlet(h):
        acc = jnp.dot(s_v[...], sc[h], preferred_element_type=F32)
        for b in range(nblk):
            x[h, b] = (acc[b * BLK:(b + 1) * BLK] * weight(b)).astype(BF)

    def update(i, h):
        e = 2 * i + 1
        wait_slabs(e, h)
        for d in range(DIRS):
            cc_copy(i, h, d).wait_recv()
            call[(d + 1) * TERMS:(d + 2) * TERMS, :] = ccr[i * CH + h, d]
        call[:TERMS, :] = ccs[i * CH + h]
        extra = jnp.dot(gg[...], call[...], preferred_element_type=F32)
        cols = slice(h * cw, (h + 1) * cw)
        for b in range(nblk):
            part = slice(b * BLK, (b + 1) * BLK)
            new = x[h, b].astype(F32) - recv[e * CH + h][code_ref[0, b]].astype(F32) + extra[part]
            if i == 0:
                res[h, part, :] = (load_v[part, cols].astype(F32) - new).astype(BF)
            else:
                new = mul[part, cols] + new
            mul[part, cols] = new

    def column_maps():
        for n in range(len(row_steps)):
            map_row[n].wait_recv()
        line = lax.broadcasted_iota(jnp.int32, (rowdev, 128), 0)
        tile = jnp.full((rowdev, 128), -1, jnp.int32)
        for n in range(rowdev):
            tile = jnp.where(line == n, mrow[n, 0:rowdev], tile)
        mtile[...] = tile
        copies = []
        for n, dz in enumerate(col_steps):
            copies.append(remote(mtile, mall.at[z], zs_sem.at[n], zr_sem.at[n], col_peer(dz)))
            copies[-1].start()
        mall[z] = tile
        started.extend(copies)
        return copies

    shift_row = (rowdev * PAD).bit_length() - 1
    shift_pad = PAD.bit_length() - 1

    def mark(dst, dofs):
        grid = jnp.transpose(dofs.astype(F32))[64:64 + PAD]
        width = dst.shape[1]
        ids = lax.broadcasted_iota(jnp.int32, (PAD, width), 1).astype(F32)
        for n in range(rows):
            hit = jnp.broadcast_to(grid[:, n:n + 1], (PAD, width)) == ids
            dst[n * PAD:(n + 1) * PAD, :] = jnp.where(hit, 1.0, 0.0).astype(BF)

    def columns(copies):
        for copy in copies:
            copy.wait_recv()
        mark(onehot, mall[...].reshape(rows, 128))
        picked = lax.dot_general(
            cinv_ref[0].astype(BF), onehot[...], (((1,), (1,)), ((), ())), preferred_element_type=F32
        ).astype(BF)
        lanes = rowdev * PAD
        copies = []
        for zz in range(zs):
            selbuf[zz] = picked[:, zz * lanes:(zz + 1) * lanes]
        for n, dz in enumerate(col_steps):
            zz = lax.rem(z + dz, zs)
            copies.append(remote(selbuf.at[zz], colz.at[z], cs_sem.at[n], cr_sem.at[n], col_peer(dz)))
            copies[-1].start()
        colz[z] = selbuf[z]
        started.extend(copies)
        return copies

    def mark_rows():
        dofs = mall[...].reshape(rows, 128)
        high = lax.shift_right_logical(dofs, shift_row)
        mid = lax.shift_right_logical(dofs, shift_pad) & (rowdev - 1)
        moved = mid * (zs * PAD) + high * PAD + (dofs & (PAD - 1))
        mark(twohot, jnp.where(dofs >= 0, moved, -1))

    def share_columns(copies):
        for copy in copies:
            copy.wait_recv()
        turned = jnp.transpose(colz[...].reshape(zs * PAD, rowdev * PAD).astype(F32)).astype(BF)
        colt[...] = turned.reshape(ys, CORES * PAD, zs * PAD)
        out = []
        for n, (dy, dc) in enumerate(row_steps):
            out.append(remote(
                colt.at[lax.rem(y + dy, ys)], colall.at[yc], ys_sem.at[n], yr_sem.at[n], row_peer(dy, dc)
            ))
            out[-1].start()
        colall[yc] = colt[y]
        started.extend(out)
        return out

    def coarse_rows(copies):
        width = CORES * PAD
        ids = lax.broadcasted_iota(jnp.int32, (half, width), 1).astype(F32)
        parts = []
        for core in range(CORES):
            table = jnp.broadcast_to(mrow[y * CORES + core, 0:1].astype(F32), (128, 128))
            want = jnp.transpose(table)[:half, :width]
            want = jnp.where(want >= 0, want + core * PAD, -1.0)
            parts.append(jnp.where(want == ids, 1.0, 0.0))
        wanted = jnp.concatenate(parts, axis=0).astype(BF)
        for copy in copies:
            copy.wait_recv()
        mat = jnp.concatenate([colall[n] for n in range(rowdev)], axis=1)
        both = lax.dot_general(
            mat, twohot[...], (((1,), (1,)), ((), ())), preferred_element_type=F32
        ).astype(BF)
        wbuf[...] = jnp.dot(wanted, both, preferred_element_type=F32).astype(BF)

    pf[...] = jnp.zeros_like(pf)
    call[...] = jnp.zeros_like(call)
    first_solve()
    for h in range(CH):
        p_fill(0, h)
        fill(0, h)
    pl.semaphore_wait(barrier, len(peers))
    for copy in map_row:
        copy.start()
    for h in range(CH):
        p_send(0, h)
    for copy in basis_out:
        copy.start()
    send(0, 0)
    map_col = column_maps()
    send(0, 1)
    col_out = columns(map_col)
    relay(0)
    mark_rows()
    row_out = share_columns(col_out)
    gain = response()
    scale(0, 0)
    dirichlet(0)
    fill(1, 0)
    send(1, 0)
    coarse_rows(row_out)
    coarse(0)
    scale(0, 1)
    dirichlet(1)
    fill(1, 1)
    for h in range(CH):
        cc_send(0, h)
    send(1, 1)
    responses(gain)
    for h in range(CH):
        update(0, h)
        solve(h)
        p_fill(1, h)
        p_send(1, h)
        fill(2, h)
    for h in range(CH):
        send(2, h)
    relay(1)
    scale(1, 0)
    dirichlet(0)
    fill(3, 0)
    send(3, 0)
    coarse(1)
    scale(1, 1)
    dirichlet(1)
    fill(3, 1)
    for h in range(CH):
        cc_send(1, h)
    send(3, 1)
    outs = []
    for h in range(CH):
        update(1, h)
        cols = pl.ds(h * cw, cw)
        outs.append(pltpu.make_async_copy(mul.at[:, cols], out_hbm.at[0, 0, :, cols], out_sem.at[h]))
        outs[-1].start()

    for copy in started:
        copy.wait_send()
    p_wait_sends()
    for i in range(ITERS):
        for n, dz in enumerate(col_steps):
            q_copy(i, n, dz).wait_send()
        partner_copy(i).wait_send()
        far_each(i, lambda copy: copy.wait_send())
    for copy in outs:
        copy.wait()


def on_device(zs, ys, gs, *args):
    (load_cases, inv_schur, schur_blocks, coarse_basis, coarse_map,
     multiplicity, recv_code, send_blocks, coarse_inv) = args
    _, _, nb, cases = load_cases.shape
    nblk = nb // BLK
    cw = cases // CH
    own, nc = coarse_inv.shape[1:]
    rowdev = ys * CORES
    rows = zs * rowdev
    tiles = nb // TILE
    dma = pltpu.SemaphoreType.DMA
    vm = pltpu.VMEM
    exchanges = 2 * ITERS * CH
    half = PAD + DIRS * 8
    sm = pltpu.SMEM
    scratch = [
        vm((1, nb), F32), vm((1, own, nc), F32), sm((1, nblk), jnp.int32), sm((1, nblk), jnp.int32),
        sm((1, nblk), jnp.int32), sm((1, SLOTS), jnp.int32), dma((6,)),
        vm((nb, cases), BF), vm((nb, nb), BF), vm((nb, nb), BF),
        dma, dma((tiles,)), dma, dma((CH,)),
        vm((nblk, BLK, BLK), F32), vm((PAD, BLK), F32),
        vm((DIRS * 8, BLK), F32), vm((DIRS * 8, BLK), F32), dma((DIRS,)), dma((DIRS,)),
        vm((8, 128), jnp.int32), vm((rowdev, 8, 128), jnp.int32), vm((rowdev, 128), jnp.int32),
        vm((zs, rowdev, 128), jnp.int32), dma((rowdev,)), dma((rowdev,)), dma((zs,)), dma((zs,)),
        vm((rows * PAD, nc), BF), vm((rows * PAD, nc), BF),
        vm((zs, own, rowdev * PAD), BF), vm((zs, own, rowdev * PAD), BF),
        vm((ys, CORES * PAD, zs * own), BF), vm((rowdev, CORES * PAD, zs * own), BF),
        dma((zs,)), dma((zs,)), dma((rowdev,)), dma((rowdev,)), vm((CORES * half, rows * PAD), BF),
        vm((CH, nblk, BLK, cw), BF), vm((exchanges, SLOTS, BLK, cw), BF),
        *[vm((SLOTS, BLK, cw), BF) for _ in range(exchanges)],
        dma((exchanges * DIRS,)), dma((exchanges * DIRS,)),
        vm((CH, nb, cw), BF), vm((nb, cases), F32), vm((CH, nb, cw), BF),
        vm((CH, PAD, cw), F32), vm((ITERS, CH, PAD, cw), BF), vm((ITERS, rowdev, PAD, cw), BF),
        vm((ITERS, zs, rowdev, PAD, cw), BF),
        dma((ITERS * CH * ys,)), dma((ITERS * rowdev,)), dma((ITERS * zs,)), dma((ITERS * zs,)),
        vm((ITERS, CORES * half, cw), F32), vm((ITERS, PAD, cw), F32), vm((CH, PAD, cw), F32),
        vm((ITERS, CH, DIRS * 8, cw), F32), vm((CH, DIRS * 8, cw), F32), dma((ITERS,)), dma((ITERS,)),
        dma((ITERS * CORES * DIRS,)), dma((ITERS * CH * DIRS,)),
        vm((nb, BLK), BF), vm((nblk, TERMS, BLK), BF), vm((SLOTS, TERMS, BLK), BF), vm((SLOTS, TERMS, BLK), BF),
        dma((DIRS,)), dma((DIRS,)), vm((nb, 2 * BLK), BF), vm((TERMS, cw), F32), vm((ITERS * CH, TERMS, cw), BF),
        vm((ITERS * CH, DIRS, TERMS, cw), BF), vm((2 * BLK, cw), BF),
        dma((ITERS * CH * DIRS,)), dma((ITERS * CH * DIRS,)),
    ]
    hbm = pl.BlockSpec(memory_space=pl.ANY)
    return pl.pallas_call(
        functools.partial(kernel, zs, ys, gs),
        out_shape=jax.ShapeDtypeStruct(load_cases.shape, F32),
        in_specs=[hbm] * 9,
        out_specs=hbm,
        scratch_shapes=scratch,
        compiler_params=pltpu.CompilerParams(
            collective_id=0, has_side_effects=True, vmem_limit_bytes=60 * 1024 * 1024
        ),
        name="feti",
    )(
        load_cases, inv_schur, schur_blocks, coarse_basis[0], coarse_inv,
        coarse_map[0], multiplicity[0], recv_code[0], send_blocks[0],
    )


def build(mesh, zs, ys):
    wide = P("group", "sub", None, None)
    thin = P("group", "sub", None)
    return jax.shard_map(
        functools.partial(on_device, zs, ys, mesh.shape["group"]),
        mesh=mesh,
        in_specs=(wide, wide, wide, thin, thin, thin, thin, thin, thin),
        out_specs=wide,
        check_vma=False,
    )


def solution(mesh):
    ys = 4
    return build(mesh, mesh.shape["sub"] // (ys * CORES), ys)
```

```python
import functools

import jax
import jax.numpy as jnp
from jax import lax
from jax.experimental import pallas as pl
from jax.experimental.pallas import tpu as pltpu
from jax.sharding import PartitionSpec as P

BLK = 128
DIRS = 6
CAP = 4
ITERS = 2
SLOTS = DIRS * CAP
PAD = 16
CH = 2
CORES = 2
TERMS = 2 * PAD
TILE = 256
OFFSETS = (1, -1, 2, -2)
ALONG = (2, 3, 0, 1)
ACROSS = (4, 5)
ORDER = ALONG + ACROSS
MESH = pl.DeviceIdType.MESH
BF = jnp.bfloat16
F32 = jnp.float32


def kernel(
    zs, ys, gs,
    load_hbm, a_hbm, s_hbm, basis_hbm, cinv_hbm, map_hbm, mult_hbm, code_hbm, send_hbm,
    out_hbm,
    basis_ref, cinv_ref, map_ref, mult_ref, code_ref, send_ref, small_sem,
    load_v, a_v, s_v, load_sem, a_sem, s_sem, out_sem,
    bcol, brow, bslab, brecv, bs_sem, br_sem,
    mown, mrow, mtile, mall, ms_sem, mr_sem, zs_sem, zr_sem,
    onehot, twohot, selbuf, colz, colt, colall, cs_sem, cr_sem, ys_sem, yr_sem, wbuf,
    x, slab, rv0, rv1, rv2, rv3, rv4, rv5, rv6, rv7, es_sem, er_sem,
    sc, mul, res,
    pf, psend, prow, pall, ps_sem, pr_sem, qs_sem, qr_sem,
    cres, cin, cloc, cfar, cnear, ks_sem, kr_sem, ts_sem, tr_sem,
    dmat, gt, gslab, grecv, gs_sem, gr_sem, gg, ccf, ccs, ccr, call, us_sem, ur_sem,
):
    nb, cases = load_v.shape
    nblk = nb // BLK
    cw = cases // CH
    rows = zs * ys * CORES
    rowdev = ys * CORES
    recv = (rv0, rv1, rv2, rv3, rv4, rv5, rv6, rv7)
    g = lax.axis_index("group")
    s = lax.axis_index("sub")
    c = lax.rem(s, CORES)
    zy = lax.div(s, CORES)
    y = lax.rem(zy, ys)
    z = lax.div(zy, ys)
    yc = y * CORES + c

    def sub_at(zz, yy, cc):
        return (zz * ys + yy) * CORES + cc

    row_ids = [[(g, sub_at(z, lax.rem(y + dy, ys), cc)) for cc in (c, 1 - c)] for dy in range(ys)]
    col_ids = [(g, sub_at(lax.rem(z + dz, zs), y, c)) for dz in range(zs)]
    near = {step: lax.rem(s - c + step + rows, rows) for step in (-2, -1, 0, 1, 2, 3)}
    sides = [lax.rem(g + step, gs) for step in (1, gs - 1)]

    def reader_of(at, core, d):
        return (g, at(core + OFFSETS[d])) if d < 4 else (sides[d - 4], at(core))

    core_readers = [[reader_of(lambda step: near[step], core, d) for d in range(DIRS)] for core in range(CORES)]
    own_readers = [
        (jnp.where(c == 0, a[0], b[0]), jnp.where(c == 0, a[1], b[1])) for a, b in zip(*core_readers)
    ]

    def row_peer(dy, dc):
        if isinstance(dc, int):
            return row_ids[dy][dc]
        here, there = row_ids[dy]
        return (g, jnp.where(dc == 0, here[1], there[1]))

    def col_peer(dz):
        return col_ids[dz]

    def reader(d, core=None):
        return own_readers[d] if core is None else core_readers[core][d]

    row_steps = [(dy, dc) for dy in range(ys) for dc in range(CORES) if (dy, dc) != (0, 0)]
    col_steps = list(range(1, zs))
    started = []

    def remote(src, dst, ssem, rsem, dev):
        return pltpu.make_async_remote_copy(
            src_ref=src, dst_ref=dst, send_sem=ssem, recv_sem=rsem,
            device_id=dev, device_id_type=MESH,
        )

    barrier = pltpu.get_barrier_semaphore()
    peers = [row_peer(dy, dc) for dy, dc in row_steps]
    peers += [col_peer(dz) for dz in col_steps]
    peers += [(g, near[step]) for step in (-2, -1, 2, 3)]
    peers += [(side, near[core]) for side in sides for core in range(CORES)]
    for peer in peers:
        pl.semaphore_signal(barrier, inc=1, device_id=peer, device_id_type=MESH)
    small = [
        pltpu.make_async_copy(src, dst, small_sem.at[n]) for n, (src, dst) in enumerate((
            (basis_hbm, basis_ref), (map_hbm, map_ref), (send_hbm, send_ref), (code_hbm, code_ref),
            (mult_hbm, mult_ref), (cinv_hbm, cinv_ref)))
    ]
    for copy in small:
        copy.start()
    load_copy = pltpu.make_async_copy(load_hbm.at[0, 0], load_v, load_sem)
    load_copy.start()
    tiles = nb // TILE

    def a_copy(t):
        part = pl.ds(t * TILE, TILE)
        return pltpu.make_async_copy(a_hbm.at[0, 0, part], a_v.at[part], a_sem.at[t])

    for t in range(tiles):
        a_copy(t).start()
    s_copy = pltpu.make_async_copy(s_hbm.at[0, 0], s_v, s_sem)
    s_copy.start()
    for copy in small:
        copy.wait()

    lane = lax.broadcasted_iota(jnp.int32, (8, 128), 1)
    mine = jnp.full((8, 128), -1, jnp.int32)
    for b in range(nblk):
        line = basis_ref[:, b * BLK:(b + 1) * BLK]
        brow[b:b + 1, :] = line
        bcol[b] = jnp.transpose(jnp.broadcast_to(line, (BLK, BLK)))
        mine = jnp.where(lane == b, b, mine)
        mine = jnp.where(lane == 64 + b, map_ref[0, b], mine)
    bslab[...] = jnp.zeros_like(bslab)
    for k in range(SLOTS):
        at = (k // CAP) * 8 + k % CAP
        block = jnp.maximum(send_ref[0, k], 0)
        mine = jnp.where(lane == PAD + at, block, mine)
        bslab[at:at + 1, :] = brow[pl.ds(block, 1), :]
    mown[...] = mine
    mrow[yc] = mine
    map_row = [
        remote(mown, mrow.at[yc], ms_sem.at[n], mr_sem.at[n], row_peer(dy, dc))
        for n, (dy, dc) in enumerate(row_steps)
    ]
    basis_out = [
        remote(bslab.at[pl.ds(d * 8, 8)], brecv.at[pl.ds(d * 8, 8)], bs_sem.at[d], br_sem.at[d], reader(d))
        for d in range(DIRS)
    ]
    started += map_row + basis_out

    def slab_copy(e, h, d):
        part = pl.ds(d * CAP, CAP)
        n = (e * CH + h) * DIRS + d
        return remote(
            slab.at[e * CH + h, part], recv[e * CH + h].at[part],
            es_sem.at[n], er_sem.at[n], reader(d),
        )

    def fill(e, h):
        for k in range(SLOTS):
            slab[e * CH + h, k] = x[h, jnp.maximum(send_ref[0, k], 0)]

    def send(e, h, dirs=ORDER):
        for d in dirs:
            copy = slab_copy(e, h, d)
            copy.start()
            started.append(copy)

    def wait_slabs(e, h):
        for d in ORDER:
            slab_copy(e, h, d).wait_recv()

    def p_fill(i, h):
        psend[i, h] = pf[h].astype(BF)

        @pl.when(c == h)
        def _():
            prow[i, yc] = pf[h].astype(BF)

    def p_send(i, h):
        dc = lax.rem(c + h, CORES)
        for dy in range(ys):
            n = (i * CH + h) * ys + dy
            copy = remote(
                psend.at[i, h], prow.at[i, yc], ps_sem.at[n],
                pr_sem.at[i * rowdev + dy * CORES + dc], row_peer(dy, dc),
            )
            if dy == 0:
                @pl.when(dc != 0)
                def _():
                    copy.start()
            else:
                copy.start()

    def p_wait_sends():
        for i in range(ITERS):
            for h in range(CH):
                dc = lax.rem(c + h, CORES)
                for dy in range(ys):
                    n = (i * CH + h) * ys + dy
                    copy = remote(
                        psend.at[i, h], prow.at[i, yc], ps_sem.at[n],
                        pr_sem.at[i * rowdev + dy * CORES + dc], row_peer(dy, dc),
                    )
                    if dy == 0:
                        @pl.when(dc != 0)
                        def _():
                            copy.wait_send()
                    else:
                        copy.wait_send()

    def q_copy(i, n, dz):
        return remote(
            prow.at[i], pall.at[i, z], qs_sem.at[i * zs + n], qr_sem.at[i * zs + n], col_peer(dz)
        )

    def relay(i):
        for dy, dc in row_steps:
            remote(
                psend.at[i, 0], prow.at[i, 0], ps_sem.at[0],
                pr_sem.at[i * rowdev + dy * CORES + dc], row_peer(dy, dc),
            ).wait_recv()
        for n, dz in enumerate(col_steps):
            q_copy(i, n, dz).start()
        pall[i, z] = prow[i]

    half = PAD + DIRS * 8

    def partner_copy(i):
        own = pl.ds((1 - c) * half, PAD)
        return remote(cres.at[i, own], cin.at[i], ks_sem.at[i], kr_sem.at[i], row_peer(0, 1))

    def far_copy(i, core, d):
        part = pl.ds(core * half + PAD + d * 8, 8)
        return remote(
            cres.at[i, part], cfar.at[i, c, pl.ds(d * 8, 8)],
            ts_sem.at[(i * CORES + core) * DIRS + d], tr_sem.at[(i * CH + c) * DIRS + d], reader(d, core),
        )

    def far_each(i, act):
        for d in range(DIRS):
            for core in range(CORES):
                if d == core:
                    @pl.when(c == core)
                    def _():
                        act(far_copy(i, core, d))
                else:
                    act(far_copy(i, core, d))

    def coarse(i):
        for n, dz in enumerate(col_steps):
            q_copy(i, n, dz).wait_recv()
        every = pall[i].reshape(rows * PAD, cw)
        cres[i] = jnp.dot(wbuf[...], every, preferred_element_type=F32)
        far_each(i, lambda copy: copy.start())
        partner_copy(i).start()
        for d in range(CORES):
            @pl.when(c != d)
            def _():
                cfar[i, c, d * 8:(d + 1) * 8, :] = cres[i, pl.ds(d * half + PAD + d * 8, 8), :]

    def collect(i, h):
        @pl.when(c == h)
        def _():
            cloc[h] = cres[i, pl.ds(h * half, PAD), :]

        @pl.when(c != h)
        def _():
            partner_copy(i).wait_recv()
            cloc[h] = cin[i]

        for d in range(DIRS):
            copy = remote(
                cres.at[i, pl.ds(0, 8)], cfar.at[i, h, pl.ds(d * 8, 8)],
                ts_sem.at[0], tr_sem.at[(i * CH + h) * DIRS + d], reader(d),
            )
            if d < CORES and d == 1 - h:
                @pl.when(c != h)
                def _():
                    copy.wait_recv()
            else:
                copy.wait_recv()
        cnear[h] = cfar[i, h]

    def code_row(b):
        code = code_ref[0, b]
        return code, (code // CAP) * 8 + code % CAP

    def weight(b):
        return 1.0 / jnp.full((1, 128), mult_ref[0, b].astype(F32))

    def keep(b, h, disp):
        pf[h, pl.ds(b, 1), :] = jnp.sum(bcol[b] * disp, axis=0, keepdims=True)
        x[h, b] = disp.astype(BF)

    per = TILE // BLK

    def first_solve():
        load_copy.wait()

        def step(t, carry):
            a_copy(t).wait()
            acc = jnp.dot(a_v[pl.ds(t * TILE, TILE), :], load_v[...], preferred_element_type=F32)
            for i in range(per):
                for h in range(CH):
                    keep(t * per + i, h, acc[i * BLK:(i + 1) * BLK, h * cw:(h + 1) * cw])
            return carry

        lax.fori_loop(0, tiles, step, 0)

    def solve(h):
        acc = jnp.dot(a_v[...], res[h], preferred_element_type=F32)
        for b in range(nblk):
            keep(b, h, acc[b * BLK:(b + 1) * BLK])

    def scale(i, h):
        e = 2 * i
        wait_slabs(e, h)

        def step(b, carry):
            code, _ = code_row(b)
            diff = x[h, b].astype(F32) - recv[e * CH + h][code].astype(F32)
            sc[h, pl.ds(b * BLK, BLK), :] = (diff * weight(b)).astype(BF)
            return carry

        lax.fori_loop(0, nblk, step, 0)

    def response():
        for copy in basis_out:
            copy.wait_recv()
        lanes = lax.broadcasted_iota(jnp.int32, (BLK, BLK), 1)
        for b in range(nblk):
            _, at = code_row(b)
            far = jnp.transpose(jnp.broadcast_to(brecv[pl.ds(at, 1), :], (BLK, BLK)))
            both = jnp.where(lanes == b, bcol[b], jnp.where(lanes == PAD + b, -far, 0.0))
            dmat[b * BLK:(b + 1) * BLK, :] = (both * weight(b)).astype(BF)
        acc = jnp.dot(s_v[...], dmat[...], preferred_element_type=F32)
        for b in range(nblk):
            turned = jnp.transpose(acc[b * BLK:(b + 1) * BLK] * weight(b))
            gt[b] = turned[:TERMS].astype(BF)
        for k in range(SLOTS):
            gslab[k] = gt[jnp.maximum(send_ref[0, k], 0)]
        copies = []
        for d in ORDER:
            part = pl.ds(d * CAP, CAP)
            copies.append(remote(gslab.at[part], grecv.at[part], gs_sem.at[d], gr_sem.at[d], reader(d)))
            copies[-1].start()
        started.extend(copies)
        return copies

    def responses(copies):
        for copy in copies:
            copy.wait_recv()
        rest = jnp.zeros((2 * BLK - (1 + DIRS) * TERMS, BLK), F32)
        for b in range(nblk):
            code, _ = code_row(b)
            far = -grecv[code].astype(F32)
            source = jnp.full(far.shape, code // CAP, jnp.int32)
            pieces = [gt[b].astype(F32)]
            pieces += [jnp.where(source == d, far, 0.0) for d in range(DIRS)] + [rest]
            wide = jnp.concatenate(pieces, axis=0)
            gg[b * BLK:(b + 1) * BLK, :BLK] = jnp.transpose(wide[:BLK]).astype(BF)
            gg[b * BLK:(b + 1) * BLK, BLK:] = jnp.transpose(wide[BLK:]).astype(BF)

    def cc_copy(i, h, d):
        n = i * CH + h
        return remote(
            ccs.at[n], ccr.at[n, d], us_sem.at[n * DIRS + d], ur_sem.at[n * DIRS + d], reader(d)
        )

    def cc_send(i, h):
        collect(i, h)
        ccf[...] = jnp.zeros_like(ccf)
        ccf[0:PAD, :] = cloc[h]
        for b in range(nblk):
            _, at = code_row(b)
            ccf[PAD + b:PAD + b + 1, :] = cnear[h, pl.ds(at, 1), :]
        ccs[i * CH + h] = ccf[...].astype(BF)
        for d in ORDER:
            copy = cc_copy(i, h, d)
            copy.start()
            started.append(copy)

    def dirichlet(h):
        acc = jnp.dot(s_v[...], sc[h], preferred_element_type=F32)
        for b in range(nblk):
            x[h, b] = (acc[b * BLK:(b + 1) * BLK] * weight(b)).astype(BF)

    def update(i, h):
        e = 2 * i + 1
        wait_slabs(e, h)
        for d in range(DIRS):
            cc_copy(i, h, d).wait_recv()
            call[(d + 1) * TERMS:(d + 2) * TERMS, :] = ccr[i * CH + h, d]
        call[:TERMS, :] = ccs[i * CH + h]
        extra = jnp.dot(gg[...], call[...], preferred_element_type=F32)
        cols = slice(h * cw, (h + 1) * cw)
        for b in range(nblk):
            part = slice(b * BLK, (b + 1) * BLK)
            new = x[h, b].astype(F32) - recv[e * CH + h][code_ref[0, b]].astype(F32) + extra[part]
            if i == 0:
                res[h, part, :] = (load_v[part, cols].astype(F32) - new).astype(BF)
            else:
                new = mul[part, cols] + new
            mul[part, cols] = new

    def column_maps():
        for n in range(len(row_steps)):
            map_row[n].wait_recv()
        line = lax.broadcasted_iota(jnp.int32, (rowdev, 128), 0)
        tile = jnp.full((rowdev, 128), -1, jnp.int32)
        for n in range(rowdev):
            tile = jnp.where(line == n, mrow[n, 0:rowdev], tile)
        mtile[...] = tile
        copies = []
        for n, dz in enumerate(col_steps):
            copies.append(remote(mtile, mall.at[z], zs_sem.at[n], zr_sem.at[n], col_peer(dz)))
            copies[-1].start()
        mall[z] = tile
        started.extend(copies)
        return copies

    shift_row = (rowdev * PAD).bit_length() - 1
    shift_pad = PAD.bit_length() - 1

    def mark(dst, dofs):
        grid = jnp.transpose(dofs.astype(F32))[64:64 + PAD]
        width = dst.shape[1]
        ids = lax.broadcasted_iota(jnp.int32, (PAD, width), 1).astype(F32)
        for n in range(rows):
            hit = jnp.broadcast_to(grid[:, n:n + 1], (PAD, width)) == ids
            dst[n * PAD:(n + 1) * PAD, :] = jnp.where(hit, 1.0, 0.0).astype(BF)

    def columns(copies):
        for copy in copies:
            copy.wait_recv()
        mark(onehot, mall[...].reshape(rows, 128))
        picked = lax.dot_general(
            cinv_ref[0].astype(BF), onehot[...], (((1,), (1,)), ((), ())), preferred_element_type=F32
        ).astype(BF)
        lanes = rowdev * PAD
        copies = []
        for zz in range(zs):
            selbuf[zz] = picked[:, zz * lanes:(zz + 1) * lanes]
        for n, dz in enumerate(col_steps):
            zz = lax.rem(z + dz, zs)
            copies.append(remote(selbuf.at[zz], colz.at[z], cs_sem.at[n], cr_sem.at[n], col_peer(dz)))
            copies[-1].start()
        colz[z] = selbuf[z]
        started.extend(copies)
        return copies

    def mark_rows():
        dofs = mall[...].reshape(rows, 128)
        high = lax.shift_right_logical(dofs, shift_row)
        mid = lax.shift_right_logical(dofs, shift_pad) & (rowdev - 1)
        moved = mid * (zs * PAD) + high * PAD + (dofs & (PAD - 1))
        mark(twohot, jnp.where(dofs >= 0, moved, -1))

    def share_columns(copies):
        for copy in copies:
            copy.wait_recv()
        turned = jnp.transpose(colz[...].reshape(zs * PAD, rowdev * PAD).astype(F32)).astype(BF)
        colt[...] = turned.reshape(ys, CORES * PAD, zs * PAD)
        out = []
        for n, (dy, dc) in enumerate(row_steps):
            out.append(remote(
                colt.at[lax.rem(y + dy, ys)], colall.at[yc], ys_sem.at[n], yr_sem.at[n], row_peer(dy, dc)
            ))
            out[-1].start()
        colall[yc] = colt[y]
        started.extend(out)
        return out

    def coarse_rows(copies):
        width = CORES * PAD
        ids = lax.broadcasted_iota(jnp.int32, (half, width), 1).astype(F32)
        parts = []
        for core in range(CORES):
            table = jnp.broadcast_to(mrow[y * CORES + core, 0:1].astype(F32), (128, 128))
            want = jnp.transpose(table)[:half, :width]
            want = jnp.where(want >= 0, want + core * PAD, -1.0)
            parts.append(jnp.where(want == ids, 1.0, 0.0))
        wanted = jnp.concatenate(parts, axis=0).astype(BF)
        for copy in copies:
            copy.wait_recv()
        mat = jnp.concatenate([colall[n] for n in range(rowdev)], axis=1)
        both = lax.dot_general(
            mat, twohot[...], (((1,), (1,)), ((), ())), preferred_element_type=F32
        ).astype(BF)
        wbuf[...] = jnp.dot(wanted, both, preferred_element_type=F32).astype(BF)

    pf[...] = jnp.zeros_like(pf)
    call[...] = jnp.zeros_like(call)
    first_solve()
    for h in range(CH):
        p_fill(0, h)
        fill(0, h)
    pl.semaphore_wait(barrier, len(peers))
    for copy in map_row:
        copy.start()
    for h in range(CH):
        p_send(0, h)
    for copy in basis_out:
        copy.start()
    send(0, 0)
    map_col = column_maps()
    send(0, 1)
    s_copy.wait()
    scale(0, 0)
    dirichlet(0)
    fill(1, 0)
    col_out = columns(map_col)
    relay(0)
    send(1, 0)
    mark_rows()
    row_out = share_columns(col_out)
    scale(0, 1)
    dirichlet(1)
    fill(1, 1)
    send(1, 1)
    gain = response()
    coarse_rows(row_out)
    coarse(0)
    for h in range(CH):
        cc_send(0, h)
    responses(gain)
    for h in range(CH):
        update(0, h)
        solve(h)
        p_fill(1, h)
        p_send(1, h)
        fill(2, h)
    for h in range(CH):
        send(2, h)
    relay(1)
    scale(1, 0)
    dirichlet(0)
    fill(3, 0)
    send(3, 0)
    coarse(1)
    scale(1, 1)
    dirichlet(1)
    fill(3, 1)
    send(3, 1)
    for h in range(CH):
        cc_send(1, h)
    outs = []
    for h in range(CH):
        update(1, h)
        cols = pl.ds(h * cw, cw)
        outs.append(pltpu.make_async_copy(mul.at[:, cols], out_hbm.at[0, 0, :, cols], out_sem.at[h]))
        outs[-1].start()

    for copy in started:
        copy.wait_send()
    p_wait_sends()
    for i in range(ITERS):
        for n, dz in enumerate(col_steps):
            q_copy(i, n, dz).wait_send()
        partner_copy(i).wait_send()
        far_each(i, lambda copy: copy.wait_send())
    for copy in outs:
        copy.wait()


def on_device(zs, ys, gs, *args):
    (load_cases, inv_schur, schur_blocks, coarse_basis, coarse_map,
     multiplicity, recv_code, send_blocks, coarse_inv) = args
    _, _, nb, cases = load_cases.shape
    nblk = nb // BLK
    cw = cases // CH
    own, nc = coarse_inv.shape[1:]
    rowdev = ys * CORES
    rows = zs * rowdev
    tiles = nb // TILE
    dma = pltpu.SemaphoreType.DMA
    vm = pltpu.VMEM
    exchanges = 2 * ITERS * CH
    half = PAD + DIRS * 8
    sm = pltpu.SMEM
    scratch = [
        vm((1, nb), F32), vm((1, own, nc), F32), sm((1, nblk), jnp.int32), sm((1, nblk), jnp.int32),
        sm((1, nblk), jnp.int32), sm((1, SLOTS), jnp.int32), dma((6,)),
        vm((nb, cases), BF), vm((nb, nb), BF), vm((nb, nb), BF),
        dma, dma((tiles,)), dma, dma((CH,)),
        vm((nblk, BLK, BLK), F32), vm((PAD, BLK), F32),
        vm((DIRS * 8, BLK), F32), vm((DIRS * 8, BLK), F32), dma((DIRS,)), dma((DIRS,)),
        vm((8, 128), jnp.int32), vm((rowdev, 8, 128), jnp.int32), vm((rowdev, 128), jnp.int32),
        vm((zs, rowdev, 128), jnp.int32), dma((rowdev,)), dma((rowdev,)), dma((zs,)), dma((zs,)),
        vm((rows * PAD, nc), BF), vm((rows * PAD, nc), BF),
        vm((zs, own, rowdev * PAD), BF), vm((zs, own, rowdev * PAD), BF),
        vm((ys, CORES * PAD, zs * own), BF), vm((rowdev, CORES * PAD, zs * own), BF),
        dma((zs,)), dma((zs,)), dma((rowdev,)), dma((rowdev,)), vm((CORES * half, rows * PAD), BF),
        vm((CH, nblk, BLK, cw), BF), vm((exchanges, SLOTS, BLK, cw), BF),
        *[vm((SLOTS, BLK, cw), BF) for _ in range(exchanges)],
        dma((exchanges * DIRS,)), dma((exchanges * DIRS,)),
        vm((CH, nb, cw), BF), vm((nb, cases), F32), vm((CH, nb, cw), BF),
        vm((CH, PAD, cw), F32), vm((ITERS, CH, PAD, cw), BF), vm((ITERS, rowdev, PAD, cw), BF),
        vm((ITERS, zs, rowdev, PAD, cw), BF),
        dma((ITERS * CH * ys,)), dma((ITERS * rowdev,)), dma((ITERS * zs,)), dma((ITERS * zs,)),
        vm((ITERS, CORES * half, cw), F32), vm((ITERS, PAD, cw), F32), vm((CH, PAD, cw), F32),
        vm((ITERS, CH, DIRS * 8, cw), F32), vm((CH, DIRS * 8, cw), F32), dma((ITERS,)), dma((ITERS,)),
        dma((ITERS * CORES * DIRS,)), dma((ITERS * CH * DIRS,)),
        vm((nb, BLK), BF), vm((nblk, TERMS, BLK), BF), vm((SLOTS, TERMS, BLK), BF), vm((SLOTS, TERMS, BLK), BF),
        dma((DIRS,)), dma((DIRS,)), vm((nb, 2 * BLK), BF), vm((TERMS, cw), F32), vm((ITERS * CH, TERMS, cw), BF),
        vm((ITERS * CH, DIRS, TERMS, cw), BF), vm((2 * BLK, cw), BF),
        dma((ITERS * CH * DIRS,)), dma((ITERS * CH * DIRS,)),
    ]
    hbm = pl.BlockSpec(memory_space=pl.ANY)
    return pl.pallas_call(
        functools.partial(kernel, zs, ys, gs),
        out_shape=jax.ShapeDtypeStruct(load_cases.shape, F32),
        in_specs=[hbm] * 9,
        out_specs=hbm,
        scratch_shapes=scratch,
        compiler_params=pltpu.CompilerParams(
            collective_id=0, has_side_effects=True, vmem_limit_bytes=60 * 1024 * 1024
        ),
        name="feti",
    )(
        load_cases, inv_schur, schur_blocks, coarse_basis[0], coarse_inv,
        coarse_map[0], multiplicity[0], recv_code[0], send_blocks[0],
    )


def build(mesh, zs, ys):
    wide = P("group", "sub", None, None)
    thin = P("group", "sub", None)
    return jax.shard_map(
        functools.partial(on_device, zs, ys, mesh.shape["group"]),
        mesh=mesh,
        in_specs=(wide, wide, wide, thin, thin, thin, thin, thin, thin),
        out_specs=wide,
        check_vma=False,
    )


def solution(mesh):
    ys = 4
    return build(mesh, mesh.shape["sub"] // (ys * CORES), ys)
```

```python
import functools

import jax
import jax.numpy as jnp
from jax import lax
from jax.experimental import pallas as pl
from jax.experimental.pallas import tpu as pltpu
from jax.sharding import PartitionSpec as P

BLK = 128
DIRS = 6
CAP = 4
ITERS = 2
SLOTS = DIRS * CAP
PAD = 16
CH = 2
CORES = 2
TERMS = 2 * PAD
TILE = 256
OFFSETS = (1, -1, 2, -2)
ALONG = (2, 3, 0, 1)
ACROSS = (4, 5)
ORDER = ALONG + ACROSS
MESH = pl.DeviceIdType.MESH
BF = jnp.bfloat16
F32 = jnp.float32


def kernel(
    zs, ys, gs,
    load_hbm, a_hbm, s_hbm, basis_hbm, cinv_hbm, map_hbm, mult_hbm, code_hbm, send_hbm,
    out_hbm,
    basis_ref, cinv_ref, map_ref, mult_ref, code_ref, send_ref, small_sem,
    load_v, a_v, s_v, load_sem, a_sem, s_sem, out_sem,
    bcol, brow, bslab, brecv, bs_sem, br_sem,
    mown, mrow, mtile, mall, ms_sem, mr_sem, zs_sem, zr_sem,
    onehot, twohot, selbuf, colz, colt, colall, cs_sem, cr_sem, ys_sem, yr_sem, wbuf,
    x, slab, rv0, rv1, rv2, rv3, rv4, rv5, rv6, rv7, es_sem, er_sem,
    sc, mul, res,
    pf, psend, prow, pall, ps_sem, pr_sem, qs_sem, qr_sem,
    cres, cin, cloc, cfar, cnear, ks_sem, kr_sem, ts_sem, tr_sem,
    dmat, gt, gslab, grecv, gs_sem, gr_sem, gg, ccf, ccs, ccr, call, us_sem, ur_sem,
):
    nb, cases = load_v.shape
    nblk = nb // BLK
    cw = cases // CH
    rows = zs * ys * CORES
    rowdev = ys * CORES
    recv = (rv0, rv1, rv2, rv3, rv4, rv5, rv6, rv7)
    g = lax.axis_index("group")
    s = lax.axis_index("sub")
    c = lax.rem(s, CORES)
    zy = lax.div(s, CORES)
    y = lax.rem(zy, ys)
    z = lax.div(zy, ys)
    yc = y * CORES + c

    def sub_at(zz, yy, cc):
        return (zz * ys + yy) * CORES + cc

    row_ids = [[(g, sub_at(z, lax.rem(y + dy, ys), cc)) for cc in (c, 1 - c)] for dy in range(ys)]
    col_ids = [(g, sub_at(lax.rem(z + dz, zs), y, c)) for dz in range(zs)]
    near = {step: lax.rem(s - c + step + rows, rows) for step in (-2, -1, 0, 1, 2, 3)}
    sides = [lax.rem(g + step, gs) for step in (1, gs - 1)]

    def reader_of(at, core, d):
        return (g, at(core + OFFSETS[d])) if d < 4 else (sides[d - 4], at(core))

    core_readers = [[reader_of(lambda step: near[step], core, d) for d in range(DIRS)] for core in range(CORES)]
    own_readers = [
        (jnp.where(c == 0, a[0], b[0]), jnp.where(c == 0, a[1], b[1])) for a, b in zip(*core_readers)
    ]

    def row_peer(dy, dc):
        if isinstance(dc, int):
            return row_ids[dy][dc]
        here, there = row_ids[dy]
        return (g, jnp.where(dc == 0, here[1], there[1]))

    def col_peer(dz):
        return col_ids[dz]

    def reader(d, core=None):
        return own_readers[d] if core is None else core_readers[core][d]

    row_steps = [(dy, dc) for dy in range(ys) for dc in range(CORES) if (dy, dc) != (0, 0)]
    col_steps = list(range(1, zs))
    started = []

    def remote(src, dst, ssem, rsem, dev):
        return pltpu.make_async_remote_copy(
            src_ref=src, dst_ref=dst, send_sem=ssem, recv_sem=rsem,
            device_id=dev, device_id_type=MESH,
        )

    barrier = pltpu.get_barrier_semaphore()
    peers = [row_peer(dy, dc) for dy, dc in row_steps]
    peers += [col_peer(dz) for dz in col_steps]
    peers += [(g, near[step]) for step in (-2, -1, 2, 3)]
    peers += [(side, near[core]) for side in sides for core in range(CORES)]
    for peer in peers:
        pl.semaphore_signal(barrier, inc=1, device_id=peer, device_id_type=MESH)
    small = [
        pltpu.make_async_copy(src, dst, small_sem.at[n]) for n, (src, dst) in enumerate((
            (basis_hbm, basis_ref), (map_hbm, map_ref), (send_hbm, send_ref), (code_hbm, code_ref),
            (mult_hbm, mult_ref), (cinv_hbm, cinv_ref)))
    ]
    for copy in small:
        copy.start()
    load_copy = pltpu.make_async_copy(load_hbm.at[0, 0], load_v, load_sem)
    load_copy.start()
    tiles = nb // TILE

    def a_copy(t):
        part = pl.ds(t * TILE, TILE)
        return pltpu.make_async_copy(a_hbm.at[0, 0, part], a_v.at[part], a_sem.at[t])

    for t in range(tiles):
        a_copy(t).start()
    s_copy = pltpu.make_async_copy(s_hbm.at[0, 0], s_v, s_sem)
    s_copy.start()
    for copy in small:
        copy.wait()

    lane = lax.broadcasted_iota(jnp.int32, (8, 128), 1)
    mine = jnp.full((8, 128), -1, jnp.int32)
    for b in range(nblk):
        line = basis_ref[:, b * BLK:(b + 1) * BLK]
        brow[b:b + 1, :] = line
        bcol[b] = jnp.transpose(jnp.broadcast_to(line, (BLK, BLK)))
        mine = jnp.where(lane == b, b, mine)
        mine = jnp.where(lane == 64 + b, map_ref[0, b], mine)
    bslab[...] = jnp.zeros_like(bslab)
    for k in range(SLOTS):
        at = (k // CAP) * 8 + k % CAP
        block = jnp.maximum(send_ref[0, k], 0)
        mine = jnp.where(lane == PAD + at, block, mine)
        bslab[at:at + 1, :] = brow[pl.ds(block, 1), :]
    mown[...] = mine
    mrow[yc] = mine
    map_row = [
        remote(mown, mrow.at[yc], ms_sem.at[n], mr_sem.at[n], row_peer(dy, dc))
        for n, (dy, dc) in enumerate(row_steps)
    ]
    basis_out = [
        remote(bslab.at[pl.ds(d * 8, 8)], brecv.at[pl.ds(d * 8, 8)], bs_sem.at[d], br_sem.at[d], reader(d))
        for d in range(DIRS)
    ]
    started += map_row + basis_out

    def slab_copy(e, h, d):
        part = pl.ds(d * CAP, CAP)
        n = (e * CH + h) * DIRS + d
        return remote(
            slab.at[e * CH + h, part], recv[e * CH + h].at[part],
            es_sem.at[n], er_sem.at[n], reader(d),
        )

    def fill(e, h):
        for k in range(SLOTS):
            slab[e * CH + h, k] = x[h, jnp.maximum(send_ref[0, k], 0)]

    def send(e, h, dirs=ORDER):
        for d in dirs:
            copy = slab_copy(e, h, d)
            copy.start()
            started.append(copy)

    def wait_slabs(e, h):
        for d in ORDER:
            slab_copy(e, h, d).wait_recv()

    def p_fill(i, h):
        psend[i, h] = pf[h].astype(BF)

        @pl.when(c == h)
        def _():
            prow[i, yc] = pf[h].astype(BF)

    def p_send(i, h):
        dc = lax.rem(c + h, CORES)
        for dy in range(ys):
            n = (i * CH + h) * ys + dy
            copy = remote(
                psend.at[i, h], prow.at[i, yc], ps_sem.at[n],
                pr_sem.at[i * rowdev + dy * CORES + dc], row_peer(dy, dc),
            )
            if dy == 0:
                @pl.when(dc != 0)
                def _():
                    copy.start()
            else:
                copy.start()

    def p_wait_sends():
        for i in range(ITERS):
            for h in range(CH):
                dc = lax.rem(c + h, CORES)
                for dy in range(ys):
                    n = (i * CH + h) * ys + dy
                    copy = remote(
                        psend.at[i, h], prow.at[i, yc], ps_sem.at[n],
                        pr_sem.at[i * rowdev + dy * CORES + dc], row_peer(dy, dc),
                    )
                    if dy == 0:
                        @pl.when(dc != 0)
                        def _():
                            copy.wait_send()
                    else:
                        copy.wait_send()

    def q_copy(i, n, dz):
        return remote(
            prow.at[i], pall.at[i, z], qs_sem.at[i * zs + n], qr_sem.at[i * zs + n], col_peer(dz)
        )

    def relay(i):
        for dy, dc in row_steps:
            remote(
                psend.at[i, 0], prow.at[i, 0], ps_sem.at[0],
                pr_sem.at[i * rowdev + dy * CORES + dc], row_peer(dy, dc),
            ).wait_recv()
        for n, dz in enumerate(col_steps):
            q_copy(i, n, dz).start()
        pall[i, z] = prow[i]

    half = PAD + DIRS * 8

    def partner_copy(i):
        own = pl.ds((1 - c) * half, PAD)
        return remote(cres.at[i, own], cin.at[i], ks_sem.at[i], kr_sem.at[i], row_peer(0, 1))

    def far_copy(i, core, d):
        part = pl.ds(core * half + PAD + d * 8, 8)
        return remote(
            cres.at[i, part], cfar.at[i, c, pl.ds(d * 8, 8)],
            ts_sem.at[(i * CORES + core) * DIRS + d], tr_sem.at[(i * CH + c) * DIRS + d], reader(d, core),
        )

    def far_each(i, act):
        for d in range(DIRS):
            for core in range(CORES):
                if d == core:
                    @pl.when(c == core)
                    def _():
                        act(far_copy(i, core, d))
                else:
                    act(far_copy(i, core, d))

    def coarse(i):
        for n, dz in enumerate(col_steps):
            q_copy(i, n, dz).wait_recv()
        every = pall[i].reshape(rows * PAD, cw)
        cres[i] = jnp.dot(wbuf[...], every, preferred_element_type=F32)
        far_each(i, lambda copy: copy.start())
        partner_copy(i).start()
        for d in range(CORES):
            @pl.when(c != d)
            def _():
                cfar[i, c, d * 8:(d + 1) * 8, :] = cres[i, pl.ds(d * half + PAD + d * 8, 8), :]

    def collect(i, h):
        @pl.when(c == h)
        def _():
            cloc[h] = cres[i, pl.ds(h * half, PAD), :]

        @pl.when(c != h)
        def _():
            partner_copy(i).wait_recv()
            cloc[h] = cin[i]

        for d in range(DIRS):
            copy = remote(
                cres.at[i, pl.ds(0, 8)], cfar.at[i, h, pl.ds(d * 8, 8)],
                ts_sem.at[0], tr_sem.at[(i * CH + h) * DIRS + d], reader(d),
            )
            if d < CORES and d == 1 - h:
                @pl.when(c != h)
                def _():
                    copy.wait_recv()
            else:
                copy.wait_recv()
        cnear[h] = cfar[i, h]

    def code_row(b):
        code = code_ref[0, b]
        return code, (code // CAP) * 8 + code % CAP

    def weight(b):
        return 1.0 / jnp.full((1, 128), mult_ref[0, b].astype(F32))

    def keep(b, h, disp):
        pf[h, pl.ds(b, 1), :] = jnp.sum(bcol[b] * disp, axis=0, keepdims=True)
        x[h, b] = disp.astype(BF)

    per = TILE // BLK

    def first_solve():
        load_copy.wait()

        def step(t, carry):
            a_copy(t).wait()
            acc = jnp.dot(a_v[pl.ds(t * TILE, TILE), :], load_v[...], preferred_element_type=F32)
            for i in range(per):
                for h in range(CH):
                    keep(t * per + i, h, acc[i * BLK:(i + 1) * BLK, h * cw:(h + 1) * cw])
            return carry

        lax.fori_loop(0, tiles, step, 0)

    def solve(h):
        acc = jnp.dot(a_v[...], res[h], preferred_element_type=F32)
        for b in range(nblk):
            keep(b, h, acc[b * BLK:(b + 1) * BLK])

    def scale(i, h):
        e = 2 * i
        wait_slabs(e, h)

        def step(b, carry):
            code, _ = code_row(b)
            diff = x[h, b].astype(F32) - recv[e * CH + h][code].astype(F32)
            sc[h, pl.ds(b * BLK, BLK), :] = (diff * weight(b)).astype(BF)
            return carry

        lax.fori_loop(0, nblk, step, 0)

    def response():
        for copy in basis_out:
            copy.wait_recv()
        lanes = lax.broadcasted_iota(jnp.int32, (BLK, BLK), 1)
        for b in range(nblk):
            _, at = code_row(b)
            far = jnp.transpose(jnp.broadcast_to(brecv[pl.ds(at, 1), :], (BLK, BLK)))
            both = jnp.where(lanes == b, bcol[b], jnp.where(lanes == PAD + b, -far, 0.0))
            dmat[b * BLK:(b + 1) * BLK, :] = (both * weight(b)).astype(BF)
        acc = jnp.dot(s_v[...], dmat[...], preferred_element_type=F32)
        for b in range(nblk):
            turned = jnp.transpose(acc[b * BLK:(b + 1) * BLK] * weight(b))
            gt[b] = turned[:TERMS].astype(BF)
        for k in range(SLOTS):
            gslab[k] = gt[jnp.maximum(send_ref[0, k], 0)]
        copies = []
        for d in ORDER:
            part = pl.ds(d * CAP, CAP)
            copies.append(remote(gslab.at[part], grecv.at[part], gs_sem.at[d], gr_sem.at[d], reader(d)))
            copies[-1].start()
        started.extend(copies)
        return copies

    def responses(copies):
        for copy in copies:
            copy.wait_recv()
        rest = jnp.zeros((2 * BLK - (1 + DIRS) * TERMS, BLK), F32)
        for b in range(nblk):
            code, _ = code_row(b)
            far = -grecv[code].astype(F32)
            source = jnp.full(far.shape, code // CAP, jnp.int32)
            pieces = [gt[b].astype(F32)]
            pieces += [jnp.where(source == d, far, 0.0) for d in range(DIRS)] + [rest]
            wide = jnp.concatenate(pieces, axis=0)
            gg[b * BLK:(b + 1) * BLK, :BLK] = jnp.transpose(wide[:BLK]).astype(BF)
            gg[b * BLK:(b + 1) * BLK, BLK:] = jnp.transpose(wide[BLK:]).astype(BF)

    def cc_copy(i, h, d):
        n = i * CH + h
        return remote(
            ccs.at[n], ccr.at[n, d], us_sem.at[n * DIRS + d], ur_sem.at[n * DIRS + d], reader(d)
        )

    def cc_send(i, h):
        collect(i, h)
        ccf[...] = jnp.zeros_like(ccf)
        ccf[0:PAD, :] = cloc[h]
        for b in range(nblk):
            _, at = code_row(b)
            ccf[PAD + b:PAD + b + 1, :] = cnear[h, pl.ds(at, 1), :]
        ccs[i * CH + h] = ccf[...].astype(BF)
        for d in ORDER:
            copy = cc_copy(i, h, d)
            copy.start()
            started.append(copy)

    def dirichlet(h):
        acc = jnp.dot(s_v[...], sc[h], preferred_element_type=F32)
        for b in range(nblk):
            x[h, b] = (acc[b * BLK:(b + 1) * BLK] * weight(b)).astype(BF)

    def update(i, h):
        e = 2 * i + 1
        wait_slabs(e, h)
        for d in range(DIRS):
            cc_copy(i, h, d).wait_recv()
            call[(d + 1) * TERMS:(d + 2) * TERMS, :] = ccr[i * CH + h, d]
        call[:TERMS, :] = ccs[i * CH + h]
        extra = jnp.dot(gg[...], call[...], preferred_element_type=F32)
        cols = slice(h * cw, (h + 1) * cw)
        for b in range(nblk):
            part = slice(b * BLK, (b + 1) * BLK)
            new = x[h, b].astype(F32) - recv[e * CH + h][code_ref[0, b]].astype(F32) + extra[part]
            if i == 0:
                res[h, part, :] = (load_v[part, cols].astype(F32) - new).astype(BF)
            else:
                new = mul[part, cols] + new
            mul[part, cols] = new

    def column_maps():
        for n in range(len(row_steps)):
            map_row[n].wait_recv()
        line = lax.broadcasted_iota(jnp.int32, (rowdev, 128), 0)
        tile = jnp.full((rowdev, 128), -1, jnp.int32)
        for n in range(rowdev):
            tile = jnp.where(line == n, mrow[n, 0:rowdev], tile)
        mtile[...] = tile
        copies = []
        for n, dz in enumerate(col_steps):
            copies.append(remote(mtile, mall.at[z], zs_sem.at[n], zr_sem.at[n], col_peer(dz)))
            copies[-1].start()
        mall[z] = tile
        started.extend(copies)
        return copies

    shift_row = (rowdev * PAD).bit_length() - 1
    shift_pad = PAD.bit_length() - 1

    def mark(dst, dofs):
        grid = jnp.transpose(dofs.astype(F32))[64:64 + PAD]
        width = dst.shape[1]
        ids = lax.broadcasted_iota(jnp.int32, (PAD, width), 1).astype(F32)
        for n in range(rows):
            hit = jnp.broadcast_to(grid[:, n:n + 1], (PAD, width)) == ids
            dst[n * PAD:(n + 1) * PAD, :] = jnp.where(hit, 1.0, 0.0).astype(BF)

    def columns(copies):
        for copy in copies:
            copy.wait_recv()
        mark(onehot, mall[...].reshape(rows, 128))
        picked = lax.dot_general(
            cinv_ref[0].astype(BF), onehot[...], (((1,), (1,)), ((), ())), preferred_element_type=F32
        ).astype(BF)
        lanes = rowdev * PAD
        copies = []
        for zz in range(zs):
            selbuf[zz] = picked[:, zz * lanes:(zz + 1) * lanes]
        for n, dz in enumerate(col_steps):
            zz = lax.rem(z + dz, zs)
            copies.append(remote(selbuf.at[zz], colz.at[z], cs_sem.at[n], cr_sem.at[n], col_peer(dz)))
            copies[-1].start()
        colz[z] = selbuf[z]
        started.extend(copies)
        return copies

    def mark_rows():
        dofs = mall[...].reshape(rows, 128)
        high = lax.shift_right_logical(dofs, shift_row)
        mid = lax.shift_right_logical(dofs, shift_pad) & (rowdev - 1)
        moved = mid * (zs * PAD) + high * PAD + (dofs & (PAD - 1))
        mark(twohot, jnp.where(dofs >= 0, moved, -1))

    def share_columns(copies):
        for copy in copies:
            copy.wait_recv()
        turned = jnp.transpose(colz[...].reshape(zs * PAD, rowdev * PAD).astype(F32)).astype(BF)
        colt[...] = turned.reshape(ys, CORES * PAD, zs * PAD)
        out = []
        for n, (dy, dc) in enumerate(row_steps):
            out.append(remote(
                colt.at[lax.rem(y + dy, ys)], colall.at[yc], ys_sem.at[n], yr_sem.at[n], row_peer(dy, dc)
            ))
            out[-1].start()
        colall[yc] = colt[y]
        started.extend(out)
        return out

    def coarse_rows(copies):
        width = CORES * PAD
        ids = lax.broadcasted_iota(jnp.int32, (half, width), 1).astype(F32)
        parts = []
        for core in range(CORES):
            table = jnp.broadcast_to(mrow[y * CORES + core, 0:1].astype(F32), (128, 128))
            want = jnp.transpose(table)[:half, :width]
            want = jnp.where(want >= 0, want + core * PAD, -1.0)
            parts.append(jnp.where(want == ids, 1.0, 0.0))
        wanted = jnp.concatenate(parts, axis=0).astype(BF)
        for copy in copies:
            copy.wait_recv()
        mat = jnp.concatenate([colall[n] for n in range(rowdev)], axis=1)
        both = lax.dot_general(
            mat, twohot[...], (((1,), (1,)), ((), ())), preferred_element_type=F32
        ).astype(BF)
        wbuf[...] = jnp.dot(wanted, both, preferred_element_type=F32).astype(BF)

    pf[...] = jnp.zeros_like(pf)
    call[...] = jnp.zeros_like(call)
    first_solve()
    for h in range(CH):
        p_fill(0, h)
        fill(0, h)
    pl.semaphore_wait(barrier, len(peers))
    for copy in map_row:
        copy.start()
    for h in range(CH):
        p_send(0, h)
    for copy in basis_out:
        copy.start()
    for h in range(CH):
        send(0, h, ACROSS)
    map_col = column_maps()
    send(0, 0, ALONG)
    col_out = columns(map_col)
    relay(0)
    send(0, 1, ALONG)
    mark_rows()
    s_copy.wait()
    scale(0, 0)
    dirichlet(0)
    fill(1, 0)
    row_out = share_columns(col_out)
    send(1, 0)
    scale(0, 1)
    dirichlet(1)
    fill(1, 1)
    send(1, 1)
    coarse_rows(row_out)
    coarse(0)
    gain = response()
    for h in range(CH):
        cc_send(0, h)
    responses(gain)
    for h in range(CH):
        update(0, h)
        solve(h)
        p_fill(1, h)
        p_send(1, h)
        fill(2, h)
        send(2, h, ORDER if h == 0 else ACROSS)
    relay(1)
    send(2, 1, ALONG)
    scale(1, 0)
    dirichlet(0)
    fill(3, 0)
    send(3, 0)
    coarse(1)
    scale(1, 1)
    dirichlet(1)
    fill(3, 1)
    send(3, 1)
    for h in range(CH):
        cc_send(1, h)
    outs = []
    for h in range(CH):
        update(1, h)
        cols = pl.ds(h * cw, cw)
        outs.append(pltpu.make_async_copy(mul.at[:, cols], out_hbm.at[0, 0, :, cols], out_sem.at[h]))
        outs[-1].start()

    for copy in started:
        copy.wait_send()
    p_wait_sends()
    for i in range(ITERS):
        for n, dz in enumerate(col_steps):
            q_copy(i, n, dz).wait_send()
        partner_copy(i).wait_send()
        far_each(i, lambda copy: copy.wait_send())
    for copy in outs:
        copy.wait()


def on_device(zs, ys, gs, *args):
    (load_cases, inv_schur, schur_blocks, coarse_basis, coarse_map,
     multiplicity, recv_code, send_blocks, coarse_inv) = args
    _, _, nb, cases = load_cases.shape
    nblk = nb // BLK
    cw = cases // CH
    own, nc = coarse_inv.shape[1:]
    rowdev = ys * CORES
    rows = zs * rowdev
    tiles = nb // TILE
    dma = pltpu.SemaphoreType.DMA
    vm = pltpu.VMEM
    exchanges = 2 * ITERS * CH
    half = PAD + DIRS * 8
    sm = pltpu.SMEM
    scratch = [
        vm((1, nb), F32), vm((1, own, nc), F32), sm((1, nblk), jnp.int32), sm((1, nblk), jnp.int32),
        sm((1, nblk), jnp.int32), sm((1, SLOTS), jnp.int32), dma((6,)),
        vm((nb, cases), BF), vm((nb, nb), BF), vm((nb, nb), BF),
        dma, dma((tiles,)), dma, dma((CH,)),
        vm((nblk, BLK, BLK), F32), vm((PAD, BLK), F32),
        vm((DIRS * 8, BLK), F32), vm((DIRS * 8, BLK), F32), dma((DIRS,)), dma((DIRS,)),
        vm((8, 128), jnp.int32), vm((rowdev, 8, 128), jnp.int32), vm((rowdev, 128), jnp.int32),
        vm((zs, rowdev, 128), jnp.int32), dma((rowdev,)), dma((rowdev,)), dma((zs,)), dma((zs,)),
        vm((rows * PAD, nc), BF), vm((rows * PAD, nc), BF),
        vm((zs, own, rowdev * PAD), BF), vm((zs, own, rowdev * PAD), BF),
        vm((ys, CORES * PAD, zs * own), BF), vm((rowdev, CORES * PAD, zs * own), BF),
        dma((zs,)), dma((zs,)), dma((rowdev,)), dma((rowdev,)), vm((CORES * half, rows * PAD), BF),
        vm((CH, nblk, BLK, cw), BF), vm((exchanges, SLOTS, BLK, cw), BF),
        *[vm((SLOTS, BLK, cw), BF) for _ in range(exchanges)],
        dma((exchanges * DIRS,)), dma((exchanges * DIRS,)),
        vm((CH, nb, cw), BF), vm((nb, cases), F32), vm((CH, nb, cw), BF),
        vm((CH, PAD, cw), F32), vm((ITERS, CH, PAD, cw), BF), vm((ITERS, rowdev, PAD, cw), BF),
        vm((ITERS, zs, rowdev, PAD, cw), BF),
        dma((ITERS * CH * ys,)), dma((ITERS * rowdev,)), dma((ITERS * zs,)), dma((ITERS * zs,)),
        vm((ITERS, CORES * half, cw), F32), vm((ITERS, PAD, cw), F32), vm((CH, PAD, cw), F32),
        vm((ITERS, CH, DIRS * 8, cw), F32), vm((CH, DIRS * 8, cw), F32), dma((ITERS,)), dma((ITERS,)),
        dma((ITERS * CORES * DIRS,)), dma((ITERS * CH * DIRS,)),
        vm((nb, BLK), BF), vm((nblk, TERMS, BLK), BF), vm((SLOTS, TERMS, BLK), BF), vm((SLOTS, TERMS, BLK), BF),
        dma((DIRS,)), dma((DIRS,)), vm((nb, 2 * BLK), BF), vm((TERMS, cw), F32), vm((ITERS * CH, TERMS, cw), BF),
        vm((ITERS * CH, DIRS, TERMS, cw), BF), vm((2 * BLK, cw), BF),
        dma((ITERS * CH * DIRS,)), dma((ITERS * CH * DIRS,)),
    ]
    hbm = pl.BlockSpec(memory_space=pl.ANY)
    return pl.pallas_call(
        functools.partial(kernel, zs, ys, gs),
        out_shape=jax.ShapeDtypeStruct(load_cases.shape, F32),
        in_specs=[hbm] * 9,
        out_specs=hbm,
        scratch_shapes=scratch,
        compiler_params=pltpu.CompilerParams(
            collective_id=0, has_side_effects=True, vmem_limit_bytes=60 * 1024 * 1024
        ),
        name="feti",
    )(
        load_cases, inv_schur, schur_blocks, coarse_basis[0], coarse_inv,
        coarse_map[0], multiplicity[0], recv_code[0], send_blocks[0],
    )


def build(mesh, zs, ys):
    wide = P("group", "sub", None, None)
    thin = P("group", "sub", None)
    return jax.shard_map(
        functools.partial(on_device, zs, ys, mesh.shape["group"]),
        mesh=mesh,
        in_specs=(wide, wide, wide, thin, thin, thin, thin, thin, thin),
        out_specs=wide,
        check_vma=False,
    )


def solution(mesh):
    ys = 4
    return build(mesh, mesh.shape["sub"] // (ys * CORES), ys)
```
